128 devices in a mesh: date: 8 (over y, core), strip: 16 (over z, x).
Axes of the slice: x: 4, y: 4, z: 4, core: 2. Of those that a mesh axis runs over, the one named last changes fastest.
Arguments:
- stack: float32 [64, 1024, 2048], P('date', 'strip'), may hold values from -6 to 6
- spatial_taps: float32 [13], replicated, may hold values from 0.2 to 1
- temporal_taps: float32 [2, 5], replicated, may hold values from -0.25 to 0.25
- foot_tile: int32 [16384], P(('date', 'strip')), may hold values from 0 to 1
- foot_row: int32 [16384], P(('date', 'strip')), may hold values from 0 to 63
- foot_count: int32 [16384], P(('date', 'strip')), may hold values from 1 to 128
- foot_owner: int32 [16384, 1], P(('date', 'strip')), may hold values from 0 to 127; in each aligned block of 128 rows (0 to 127, 128 to 255, ...) at most 2 rows name the same one
Outputs:
- residual: float32 [64, 1024, 2048], P(None, 'strip', 'date')
- anomaly: float32 [128, 256, 64], P(('date', 'strip'))
- asset_series: float32 [128, 64], P(('date', 'strip'))
The draws below stay inside these ranges and needn't reach their ends.
Inputs may be any that keep to these rules, and one draw needn't show every extreme that they name: `foot_owner`: among the footprints of one block, no owner appears more than 2 times, a bound that some block reaches; every owner has some footprint.
All inputs are finite; a program needn't handle non-finite values.
Results may differ from the reference program's by a relative error of at most 0.000075.
Values sent between devices are 32-bit elements; how exact they have to be, the bound alone decides.
A program may use at most 128 MiB of HBM per device.

```python
import math
import jax
import jax.numpy as jnp
import numpy as np
from jax import lax

DATES = 64
ROW_DEV = 64
TILE = 128
RADIUS = 6
REACH = 2
DILATION = 8
PAIR_CAP = 2
ROWS = 1024
COLS = 2048
TILE_DEV = 2
FOOT_DEV = 128
FOOTS = 16384
N_DATE = 8
N_STRIP = 16
DEVICES = 128


def place_ends(entries, stream_key, smallest, high):
    extent = entries.shape
    place = [jax.random.randint(jax.random.fold_in(stream_key, axis), (), 0, extent[axis]) for axis in range(len(extent))]
    entries = entries.at[tuple(place)].set(smallest)
    longest = extent.index(max(extent))
    place[longest] = (place[longest] + 1) % extent[longest]
    return entries.at[tuple(place)].set(high)


def shard_levels(own_key, shape, shards, low, top_value):
    level = 1.0
    for dim, shards_of in shards:
        draws = jax.random.uniform(jax.random.fold_in(jax.random.fold_in(own_key, 6), dim), (shards_of,), jnp.float32, low / len(shards), top_value / len(shards))
        level = level * jnp.repeat(jnp.exp(draws), shape[dim] // shards_of).reshape((-1,) + (1,) * (len(shape) - 1 - dim))
    return level


def deal_out(own_key, own, number, rows, count, top, limit, lean):
    sequence = jax.random.permutation(own_key, count)
    heavy_load, common = portions_of(count, rows * top, limit, lean, True), portions_of(count, rows * top, limit, lean, False)
    places = jnp.arange(count)

    def named(sizes, rotation):
        used = int((sizes > 0).sum())
        fixed = max(1, used // 4)
        moved = fixed + (places - fixed + rotation * (used - fixed)) % max(1, count - fixed)
        return jnp.zeros((count,), jnp.int32).at[sequence[jnp.where(places < fixed, places, moved)]].set(jnp.asarray(sizes, jnp.int32))

    sizes = jnp.where(number % 4 == 0, named(heavy_load, number // 4), named(common, number - number // 4 - 1))
    mixed = jax.random.permutation(jax.random.fold_in(own, 3), count)
    giver, taker = mixed[0:count // 2 * 2:2], mixed[1:count // 2 * 2:2]
    room = jnp.minimum(sizes[giver] - 1, limit - sizes[taker]) // 2
    room = jnp.where((giver == sequence[0]) | (taker == sequence[0]) | (sizes[taker] == 0), 0, jnp.maximum(room, 0))
    moved = jax.random.randint(jax.random.fold_in(own, 4), (count // 2,), 0, 1 << 20) % (room + 1)
    sizes = sizes.at[giver].add(-moved).at[taker].add(moved)
    labels = jnp.searchsorted(jnp.cumsum(sizes), jnp.arange(rows * top), side="right").astype(jnp.int32)
    listing = labels.reshape(top, rows).T
    listing = listing[jax.random.permutation(jax.random.fold_in(own, 1), rows)]
    rotation = jax.random.randint(jax.random.fold_in(own, 2), (rows, 1), 0, top)
    return jnp.take_along_axis(listing, (jnp.arange(top)[None, :] + rotation) % top, axis=1)


def portions_of(count, total, reach, skew, full):
    weights = [(1 << 20) // math.isqrt(rank ** skew) + 1 for rank in range(1, count + 1)]
    largest = reach if full else min(reach, max(-(-total // count), total * weights[0] // sum(weights)))
    least = 1 if total - largest >= count - 1 else 0
    given, surplus = [largest] + [least] * (count - 1), total - largest - least * (count - 1)
    while surplus > 0:
        movable = [i for i in range(1, count) if given[i] < largest] or [i for i in range(1, count) if given[i] < reach]
        whole, left = sum([weights[i] for i in movable]), surplus
        for i in movable:
            more = min(reach - given[i], max(1, left * weights[i] // whole), surplus)
            given[i] = given[i] + more
            surplus = surplus - more
    return np.array(given)


def normal_values(own_key, extent, width, limit, split=(), kind=jnp.bfloat16):
    factor_of = shard_levels(own_key, extent, split, -0.22, 0.18) if split else 1.0
    values = jax.random.normal(own_key, extent, jnp.float32) * width * factor_of
    return jnp.minimum(jnp.maximum(values, -limit), limit).astype(kind)


def setup_inputs(seed: int = 0) -> dict:
    key_of = jax.random.split(jax.random.key(seed), 8)
    stack = normal_values(key_of[0], (DATES, ROWS, COLS), 1.0, 6.0, ((0, 8), (1, 16)), jnp.float32)
    spatial_taps = jnp.clip(jnp.exp(jax.random.uniform(key_of[1], (2 * RADIUS + 1,), jnp.float32, math.log(0.2), math.log(1.0))), 0.2, 1.0)
    temporal_taps = jnp.clip(jax.random.uniform(key_of[2], (2, 2 * REACH + 1), jnp.float32, -0.25, 0.25), -0.25, 0.25)
    foot_tile = place_ends(jax.random.randint(key_of[3], (FOOTS,), 0, TILE_DEV), jax.random.fold_in(key_of[3], 1), 0, TILE_DEV - 1).astype(jnp.int32)
    foot_row = place_ends(jax.random.randint(key_of[4], (FOOTS,), 0, ROW_DEV), jax.random.fold_in(key_of[4], 1), 0, ROW_DEV - 1).astype(jnp.int32)
    foot_count = place_ends(jax.random.randint(key_of[5], (FOOTS,), 1, TILE + 1), jax.random.fold_in(key_of[5], 1), 1, TILE).astype(jnp.int32)
    foot_owner_keys = jax.random.split(jax.random.fold_in(key_of[6], 1), FOOTS // FOOT_DEV)
    foot_owner_turns = jax.random.permutation(jax.random.fold_in(key_of[6], 3), FOOTS // FOOT_DEV)
    foot_owner = jax.vmap(lambda own, number: deal_out(jax.random.fold_in(key_of[6], 2), own, number, FOOT_DEV, DEVICES, 1, PAIR_CAP, 2))(foot_owner_keys, foot_owner_turns).reshape((FOOTS, 1))
    return dict(stack=stack, spatial_taps=spatial_taps, temporal_taps=temporal_taps, foot_tile=foot_tile, foot_row=foot_row, foot_count=foot_count, foot_owner=foot_owner)


def taps_pass(padded, weights, axis_num, length):
    summed = weights[0] * lax.slice_in_dim(padded, 0, length, axis=axis_num)
    for k in range(1, weights.shape[0]):
        summed = summed + weights[k] * lax.slice_in_dim(padded, k, k + length, axis=axis_num)
    return summed


def lowpass_image(image, weights):
    row_count, col_count = image.shape
    padded = jnp.pad(image, ((0, 0), (RADIUS, RADIUS)))
    across = taps_pass(padded, weights, 1, col_count)
    padded = jnp.pad(across, ((RADIUS, RADIUS), (0, 0)))
    return image - taps_pass(padded, weights, 0, row_count)


def temporal_filter(series, temporal_taps):
    date_count = series.shape[0]
    for level_idx, spacing in enumerate((1, DILATION)):
        margin = REACH * spacing
        padded = jnp.pad(series, ((margin, margin), (0, 0), (0, 0)))
        smooth_part = temporal_taps[level_idx, 0] * lax.slice_in_dim(padded, 0, date_count, axis=0)
        for k in range(1, 2 * REACH + 1):
            smooth_part = smooth_part + temporal_taps[level_idx, k] * lax.slice_in_dim(padded, k * spacing, k * spacing + date_count, axis=0)
        series = series - smooth_part
    return series


def reference(stack, spatial_taps, temporal_taps, foot_tile, foot_row, foot_count, foot_owner):
    weights = spatial_taps / jnp.sum(spatial_taps)
    corrected = lax.map(lambda image: lowpass_image(image, weights), stack)
    banded = jnp.moveaxis(corrected.reshape(DATES, N_STRIP, ROW_DEV, COLS), 1, 0)
    filtered = lax.map(lambda block: temporal_filter(block, temporal_taps), banded)
    residual = jnp.moveaxis(filtered, 0, 1).reshape(DATES, ROWS, COLS)
    devices_all = N_DATE * N_STRIP
    block_ids = jnp.arange(FOOT_DEV * devices_all, dtype=jnp.int32) // FOOT_DEV
    band_ids = block_ids % N_STRIP
    column_ids = block_ids // N_STRIP
    tile_view = residual.reshape(DATES, N_STRIP, ROW_DEV, N_DATE, TILE_DEV, TILE)
    picked = tile_view[:, band_ids, foot_row, column_ids, foot_tile, :]
    counts = foot_count.astype(jnp.float32)
    inside = (jnp.arange(TILE, dtype=jnp.int32)[None, :] < foot_count[:, None]).astype(jnp.float32)
    foot_mean = jnp.sum(picked * inside[None], axis=2) / counts[None, :]
    owners = foot_owner[:, 0].reshape(devices_all, FOOT_DEV)
    position = jnp.arange(FOOT_DEV, dtype=jnp.int32)
    earlier = (owners[:, :, None] == owners[:, None, :]) & (position[None, None, :] < position[None, :, None])
    slot_rank = jnp.sum(earlier.astype(jnp.int32), axis=2)
    dest_slot = owners * PAIR_CAP + slot_rank
    onehot = (dest_slot[:, :, None] == jnp.arange(devices_all * PAIR_CAP, dtype=jnp.int32)[None, None, :]).astype(jnp.float32)
    series_blocks = foot_mean.reshape(DATES, devices_all, FOOT_DEV)
    sent = jnp.einsum("bfk,tbf->bkt", onehot, series_blocks, precision=lax.Precision.HIGHEST)
    sent_weight = jnp.einsum("bfk,bf->bk", onehot, counts.reshape(devices_all, FOOT_DEV), precision=lax.Precision.HIGHEST)
    received = jnp.transpose(sent.reshape(devices_all, devices_all, PAIR_CAP, DATES), (1, 0, 2, 3))
    weight_in = jnp.transpose(sent_weight.reshape(devices_all, devices_all, PAIR_CAP), (1, 0, 2))
    total_weight = jnp.sum(weight_in, axis=(1, 2))
    asset_series = jnp.sum(weight_in[:, :, :, None] * received, axis=(1, 2)) / total_weight[:, None]
    anomaly = jnp.where(weight_in[:, :, :, None] > 0, received - asset_series[:, None, None, :], 0.0)
    return residual, anomaly.reshape(devices_all, devices_all * PAIR_CAP, DATES), asset_series
```

```python
import functools
import jax
import jax.numpy as jnp
from jax import lax
from jax.experimental import pallas as pl
from jax.experimental.pallas import tpu as pltpu
from jax.sharding import PartitionSpec as P

MESH = pl.DeviceIdType.MESH
F32, BF16, I32 = jnp.float32, jnp.bfloat16, jnp.int32
ND, NS = 8, 16
T, TL = 64, 8
R, G = 64, 8
C, CB = 2048, 256
F = 128
RAD = 6
HELD = 2


def dot(a, b):
    return jnp.dot(a, b, preferred_element_type=F32)


def split(x):
    hi = x.astype(BF16)
    return hi, (x - hi.astype(F32)).astype(BF16)


def iota(shape, dim):
    return lax.broadcasted_iota(I32, shape, dim)


def kernel(
    stack, spat, temp, ftile, frow, fcount, fowner,
    res_out, anom_out, asset_out,
    win, rp, b0h, b0l, b1h, b1l, sbuf, rbuf, fbuf,
    mloc, mall, out_t, cnt_t, cnt_o, obuf, st1, wh, wl, y2, z2, zz, abuf, asbuf,
    win_sem, ml_sem, halo_s, halo_r, meta_s, meta_r, bulk_s, bulk_r,
    st1_s, st1_r, st2_s, st2_r, out_sem, fin_sem,
):
    d = lax.axis_index("date")
    s = lax.axis_index("strip")

    bar = pltpu.get_barrier_semaphore()
    for k in range(1, ND):
        pl.semaphore_signal(bar, inc=1, device_id=((d + k) % ND, s), device_id_type=MESH)
    for k in range(1, NS):
        pl.semaphore_signal(bar, inc=1, device_id=(d, (s + k) % NS), device_id_type=MESH)

    def window(g):
        lo, hi = max(8 * g - 8, 0), min(8 * g + 16, R)
        at = lo - (8 * g - 8)
        return pltpu.make_async_copy(
            stack.at[:, lo:hi, :], win.at[g, :, at : at + hi - lo, :], win_sem.at[g]
        )

    order = [(i + 1) % G for i in range(G)]
    for g in order:
        window(g).start()
    metas = [
        pltpu.make_async_copy(ref, mloc.at[i], ml_sem.at[i])
        for i, ref in enumerate((ftile, frow, fcount, fowner))
    ]
    for cp in metas:
        cp.start()

    total = spat[0]
    for k in range(1, 2 * RAD + 1):
        total = total + spat[k]
    tot = jnp.full((8, CB), total, F32)
    scale = 1.0 / (tot * tot)
    for q in range(CB // 8):
        row = iota((8, CB), 0) + 8 * q
        col = iota((8, CB), 1)
        main = row - col + RAD
        edge = jnp.where(row < 128, row - 128, row + 128) - col + RAD
        vm, ve = jnp.zeros((8, CB), F32), jnp.zeros((8, CB), F32)
        has_edge = 120 <= 8 * q < 136
        for k in range(2 * RAD + 1):
            vm = jnp.where(main == k, spat[k], vm)
            if has_edge:
                ve = jnp.where(edge == k, spat[k], ve)
        fbuf[q] = vm * scale
        fbuf[32 + q] = ve * scale
    h, l = split(fbuf[0:32].reshape(CB, CB))
    b0h[...], b0l[...] = h, l
    h, l = split(fbuf[32:64].reshape(CB, CB))
    b1h[...], b1l[...] = h, l
    rp[0] = jnp.zeros((TL, 8, CB), F32)
    rp[ND + 1] = jnp.zeros((TL, 8, CB), F32)

    def filter_chunk(g):
        def row_pass(t, carry):
            for p in range(ND):
                cols = slice(p * CB, (p + 1) * CB)
                acc = spat[0] * win[g, t, 2:10, cols]
                for k in range(1, 2 * RAD + 1):
                    acc = acc + spat[k] * win[g, t, 2 + k : 10 + k, cols]
                rp[p + 1, t] = acc
            return carry

        lax.fori_loop(0, TL, row_pass, 0)
        x = rp[1 : ND + 1].reshape(ND * TL * 8, CB)
        xh, xl = split(x)
        low = dot(xh, b0h[...]) + dot(xl, b0h[...]) + dot(xh, b0l[...])
        e = jnp.concatenate([rp[0:ND, :, :, 128:], rp[2 : ND + 2, :, :, :128]], axis=-1)
        eh, el = split(e.reshape(ND * TL * 8, CB))
        low = low + dot(eh, b1h[...]) + dot(el, b1h[...]) + dot(eh, b1l[...])
        low = low.reshape(ND, TL, 8, CB)
        for p in range(ND):
            sbuf[p, g] = win[g, :, 8:16, p * CB : (p + 1) * CB] - low[p]
        rbuf[g, pl.ds(TL * d, TL)] = sbuf[d, g]

    def bulk(g, k):
        p = (d + k) % ND
        return pltpu.make_async_remote_copy(
            src_ref=sbuf.at[p, g],
            dst_ref=rbuf.at[g, pl.ds(TL * d, TL)],
            send_sem=bulk_s.at[g, k],
            recv_sem=bulk_r.at[g, k],
            device_id=(p, s),
            device_id_type=MESH,
        )

    def send_chunk(g):
        for k in range(1, ND):
            bulk(g, k).start()

    def halo(down):
        src = stack.at[:, R - 8 : R, :] if down else stack.at[:, 0:8, :]
        dst = win.at[0, :, 0:8, :] if down else win.at[G - 1, :, 16:24, :]
        i = 0 if down else 1
        to = (s + 1) % NS if down else (s + NS - 1) % NS
        return pltpu.make_async_remote_copy(
            src_ref=src, dst_ref=dst, send_sem=halo_s.at[i], recv_sem=halo_r.at[i],
            device_id=(d, to), device_id_type=MESH,
        )

    def meta(k):
        return pltpu.make_async_remote_copy(
            src_ref=mloc, dst_ref=mall.at[d], send_sem=meta_s.at[k], recv_sem=meta_r.at[k],
            device_id=((d + k) % ND, s), device_id_type=MESH,
        )

    def wait_window(g):
        pltpu.make_async_copy(stack.at[:, 0:24, :], win.at[g], win_sem.at[g]).wait()

    wait_window(order[0])
    filter_chunk(order[0])
    pl.semaphore_wait(bar, ND - 1 + NS - 1)
    send_chunk(order[0])
    halo(True).start()
    halo(False).start()
    for cp in metas:
        cp.wait()
    for k in range(1, ND):
        meta(k).start()

    def interior(g, carry):
        wait_window(g)
        filter_chunk(g)
        send_chunk(g)
        return carry

    lax.fori_loop(2, G - 1, interior, 0)

    r_, c_ = iota((T, T), 0), iota((T, T), 1)
    r2, c2 = iota((T, 2 * T), 0), iota((T, 2 * T), 1) % T
    near = jnp.where(r_ == c_, 1.0, 0.0).astype(F32)
    far = jnp.where(r2 == c2, 1.0, 0.0).astype(F32)
    for k in range(5):
        near = near - jnp.where(r_ - c_ == k - 2, temp[0, k], 0.0)
        far = far - jnp.where(r2 - c2 == 8 * (k - 2), temp[1, k], 0.0)
    tt = jnp.dot(near, far, precision=lax.Precision.HIGHEST, preferred_element_type=F32)
    wh[...] = jnp.zeros(wh.shape, BF16)
    wl[...] = jnp.zeros(wl.shape, BF16)
    half = iota((8, 2 * T), 1) < T
    for i in range(ND):
        part = tt[8 * i : 8 * i + 8]
        base = jnp.concatenate([jnp.where(half, part, 0.0), jnp.where(half, 0.0, part)], axis=0)
        bh, bl = split(base)
        for p in range(ND):
            wh[i * 128 + 16 * p : i * 128 + 16 * p + 16, 128 * p : 128 * p + 128] = bh
            wl[i * 128 + 16 * p : i * 128 + 16 * p + 16, 128 * p : 128 * p + 128] = bl

    halo(True).wait()
    halo(False).wait()
    for g in (0, G - 1):
        window(g).wait()

    @pl.when(s == 0)
    def _():
        win[0, :, 0:8, :] = jnp.zeros((TL, 8, C), F32)

    @pl.when(s == NS - 1)
    def _():
        win[G - 1, :, 16:24, :] = jnp.zeros((TL, 8, C), F32)

    def edge_chunk(i, carry):
        filter_chunk((G - 1) * i)
        return carry

    lax.fori_loop(0, 2, edge_chunk, 0)

    mall[d] = mloc[...]
    for k in range(1, ND):
        meta(k).wait()
    cnt_t[...] = jnp.zeros(cnt_t.shape, F32)

    def block(p, carry):
        tile, row, count, owner = (mall[p, i] for i in range(4))
        jj = iota((CB, F), 0)
        inside = ((jj >> 7) == tile) & ((jj & 127) < count)
        m = jnp.where(inside, 1.0, 0.0).astype(BF16)
        xh, xl = split(sbuf[p].reshape(G * TL * 8, CB))
        g_ = (dot(xh, m) + dot(xl, m)).reshape(G, TL, 8, F)
        here = iota((G, 8, F), 0) * 8 + iota((G, 8, F), 1) == row.reshape(1, 1, F)
        picked = jnp.sum(jnp.where(here[:, None], g_, 0.0), axis=0)
        cf = count.astype(F32)
        mean = jnp.sum(picked, axis=1) / cf
        own = jnp.broadcast_to(owner.astype(F32), (F, F))
        own_t = own.T
        sub, lane = iota((F, F), 0), iota((F, F), 1)
        earlier = (own == own_t) & (sub < lane)
        slot = jnp.sum(jnp.where(earlier, 1.0, 0.0), axis=0, keepdims=True)
        onehot = jnp.where(own_t == lane.astype(F32), 1.0, 0.0)
        rows = jnp.concatenate(
            [
                jnp.where(slot == 0.0, mean, 0.0),
                jnp.where(slot == 1.0, mean, 0.0),
                jnp.where(iota((8, F), 0).astype(F32) == slot, cf, 0.0),
            ],
            axis=0,
        )
        got = jnp.dot(rows, onehot, precision=lax.Precision.HIGHEST, preferred_element_type=F32)
        out_t[pl.ds(pl.multiple_of(16 * p, 16), 16)] = got[0:16]
        cnt_t[pl.ds(pl.multiple_of(8 * p, 8), 8)] = got[16:24]
        return carry

    lax.fori_loop(0, ND, block, 0)
    obuf[...] = out_t[...].T
    cnt_o[...] = cnt_t[...].T

    def stage1(k):
        p = (d + k) % ND
        return pltpu.make_async_remote_copy(
            src_ref=obuf.at[pl.ds(pl.multiple_of(16 * p, 16), 16)], dst_ref=st1.at[d],
            send_sem=st1_s.at[k], recv_sem=st1_r.at[k],
            device_id=(p, s), device_id_type=MESH,
        )

    for k in range(1, ND):
        stage1(k).start()
    mine = pl.ds(pl.multiple_of(16 * d, 16), 16)
    st1[d] = obuf[mine]
    send_chunk(0)
    send_chunk(G - 1)

    ca = [-temp[0, k] for k in range(5)]
    cb = [-temp[1, k] for k in range(5)]
    ca[2], cb[2] = 1.0 + ca[2], 1.0 + cb[2]

    def finish_chunk(g):
        for k in range(1, ND):
            bulk(g, k).wait()

        def level(src, dst, coef, step):
            for t in range(T):
                acc = coef[2] * src(t)
                for k in (0, 1, 3, 4):
                    u = t + step * (k - 2)
                    if 0 <= u < T:
                        acc = acc + coef[k] * src(u)
                dst(t, acc)

        def put_f(t, v):
            fbuf[t] = v

        def put_r(t, v):
            rbuf[g, t] = v

        level(lambda t: rbuf[g, t], put_f, ca, 1)
        level(lambda t: fbuf[t], put_r, cb, 8)
        result(g).start()

    def result(g):
        return pltpu.make_async_copy(
            rbuf.at[g],
            res_out.at[:, pl.ds(pl.multiple_of(8 * g, 8), 8), :],
            out_sem.at[g],
        )

    def finish(g, carry):
        finish_chunk(g)
        return carry

    lax.fori_loop(1, G - 1, finish, 0)

    for k in range(1, ND):
        stage1(k).wait()
    ser = jnp.concatenate([st1[i] for i in range(ND)], axis=-1)
    sh, sl = split(ser)
    y = dot(sh, wh[...]) + dot(sl, wh[...]) + dot(sh, wl[...])
    cnt = cnt_o[mine]
    for i in range(NS):
        y2[i, :, 0 : 8 * F] = y[i : i + 1]
        y2[i, :, 8 * F : 9 * F] = cnt[i : i + 1]

    def stage2(k):
        o = (s + k) % NS
        return pltpu.make_async_remote_copy(
            src_ref=y2.at[o], dst_ref=z2.at[s],
            send_sem=st2_s.at[k], recv_sem=st2_r.at[k],
            device_id=(d, o), device_id_type=MESH,
        )

    for k in range(1, NS):
        stage2(k).start()
    z2[s] = y2[s]

    lax.fori_loop(0, 1, finish, 0)

    for k in range(1, NS):
        stage2(k).wait()
    for i in range(NS):
        zz[i : i + 1] = z2[i]
    z, cn = zz[:, 0 : 8 * F], zz[:, 8 * F : 9 * F]
    spread = jnp.where(
        iota((F, 8 * F), 0) == (iota((F, 8 * F), 1) // F) * 8 + (iota((F, 8 * F), 1) % F) // T, 1.0, 0.0
    ).astype(BF16)
    weight = dot(cn.astype(BF16), spread)
    part = jnp.sum(weight * z, axis=0, keepdims=True)
    acc = part[:, 0:F]
    for i in range(1, ND):
        acc = acc + part[:, i * F : (i + 1) * F]
    acc = acc + jnp.concatenate([acc[:, T:], acc[:, :T]], axis=1)
    asset = acc / jnp.sum(cn)
    for i in range(ND):
        cols = slice(i * F, (i + 1) * F)
        abuf[16 * i : 16 * i + 16] = jnp.where(weight[:, cols] > 0, z[:, cols] - asset, 0.0)
    asbuf[...] = asset
    ends = [
        pltpu.make_async_copy(abuf, anom_out, fin_sem.at[0]),
        pltpu.make_async_copy(asbuf, asset_out, fin_sem.at[1]),
    ]
    for cp in ends:
        cp.start()

    lax.fori_loop(G - 1, G, finish, 0)
    for cp in ends:
        cp.wait()
    for g in range(G):
        result(g).wait()


def shards(stack, spatial_taps, temporal_taps, foot_tile, foot_row, foot_count, foot_owner):
    anywhere, smem = pl.BlockSpec(memory_space=pl.ANY), pl.BlockSpec(memory_space=pltpu.SMEM)
    vm, dma = pltpu.VMEM, pltpu.SemaphoreType.DMA
    scratch = [
        vm((G, TL, 24, C), F32), vm((ND + 2, TL, 8, CB), F32),
        vm((CB, CB), BF16), vm((CB, CB), BF16), vm((CB, CB), BF16), vm((CB, CB), BF16),
        vm((ND, G, TL, 8, CB), F32), vm((G, T, 8, CB), F32), vm((T, 8, CB), F32),
        vm((4, 1, F), I32), vm((ND, 4, 1, F), I32),
        vm((F, F), F32), vm((F, F), F32), vm((F, F), F32), vm((F, F), F32),
        vm((ND, NS, F), F32), vm((8 * F, 8 * F), BF16), vm((8 * F, 8 * F), BF16),
        vm((NS, 1, 9 * F), F32), vm((NS, 1, 9 * F), F32), vm((NS, 9 * F), F32),
        vm((F, F), F32), vm((1, F), F32),
        dma((G,)), dma((4,)), dma((2,)), dma((2,)), dma((ND,)), dma((ND,)),
        dma((G, ND)), dma((G, ND)), dma((ND,)), dma((ND,)), dma((NS,)), dma((NS,)),
        dma((G,)), dma((2,)),
    ]
    residual, anomaly, asset = pl.pallas_call(
        kernel,
        out_shape=(
            jax.ShapeDtypeStruct((T, R, CB), F32),
            jax.ShapeDtypeStruct((F, F), F32),
            jax.ShapeDtypeStruct((1, F), F32),
        ),
        in_specs=[anywhere, smem, smem, anywhere, anywhere, anywhere, anywhere],
        out_specs=(anywhere, anywhere, anywhere),
        scratch_shapes=scratch,
        compiler_params=pltpu.CompilerParams(
            collective_id=0, has_side_effects=True, vmem_limit_bytes=60 << 20
        ),
        name="series",
    )(
        stack, spatial_taps, temporal_taps, foot_tile.reshape(1, F), foot_row.reshape(1, F),
        foot_count.reshape(1, F), foot_owner.reshape(1, F),
    )
    return residual, anomaly.reshape(1, 2 * F, T), asset[:, :T]


def solution(mesh):
    rows = P(("date", "strip"))
    return jax.shard_map(
        shards,
        mesh=mesh,
        in_specs=(P("date", "strip", None), P(), P(), rows, rows, rows, P(("date", "strip"), None)),
        out_specs=(P(None, "strip", "date"), P(("date", "strip"), None, None), P(("date", "strip"), None)),
        check_vma=False,
    )
```

```python
import functools
import jax
import jax.numpy as jnp
from jax import lax
from jax.experimental import pallas as pl
from jax.experimental.pallas import tpu as pltpu
from jax.sharding import PartitionSpec as P

MESH = pl.DeviceIdType.MESH
F32, BF16, I32 = jnp.float32, jnp.bfloat16, jnp.int32
ND, NS = 8, 16
T, TL = 64, 8
R, G = 64, 8
C, CB = 2048, 256
F = 128
RAD = 6
HELD = 2


def dot(a, b):
    return jnp.dot(a, b, preferred_element_type=F32)


def split(x):
    hi = x.astype(BF16)
    return hi, (x - hi.astype(F32)).astype(BF16)


def iota(shape, dim):
    return lax.broadcasted_iota(I32, shape, dim)


def filter_dates(src, mid, dst, temp):
    ca = [-temp[0, k] for k in range(5)]
    cb = [-temp[1, k] for k in range(5)]
    ca[2], cb[2] = 1.0 + ca[2], 1.0 + cb[2]
    for a, b, coef, step in ((src, mid, ca, 1), (mid, dst, cb, 8)):
        for t in range(T):
            acc = coef[2] * a[t]
            for k in (0, 1, 3, 4):
                u = t + step * (k - 2)
                if 0 <= u < T:
                    acc = acc + coef[k] * a[u]
            b[t] = acc


def kernel(
    stack, spat, temp, ftile, frow, fcount, fowner,
    gat_out, anom_out, asset_out,
    win, rp, b0h, b0l, b1h, b1l, sbuf, rbuf, fbuf,
    mloc, mall, out_t, cnt_t, cnt_o, obuf, st1, wh, wl, y2, z2, zz, xbuf, abuf, asbuf,
    win_sem, ml_sem, halo_s, halo_r, meta_s, meta_r, bulk_s, bulk_r,
    st1_s, st1_r, st2_s, st2_r, keep_sem, out_sem, fin_sem,
):
    d = lax.axis_index("date")
    s = lax.axis_index("strip")

    bar = pltpu.get_barrier_semaphore()
    for k in range(1, ND):
        pl.semaphore_signal(bar, inc=1, device_id=((d + k) % ND, s), device_id_type=MESH)
    for k in range(1, NS):
        pl.semaphore_signal(bar, inc=1, device_id=(d, (s + k) % NS), device_id_type=MESH)

    def window(g):
        lo, hi = max(8 * g - 8, 0), min(8 * g + 16, R)
        at = lo - (8 * g - 8)
        return pltpu.make_async_copy(
            stack.at[:, lo:hi, :], win.at[g, :, at : at + hi - lo, :], win_sem.at[g]
        )

    order = [(i + 1) % G for i in range(G)]
    for g in order:
        window(g).start()
    metas = [
        pltpu.make_async_copy(ref, mloc.at[i], ml_sem.at[i])
        for i, ref in enumerate((ftile, frow, fcount, fowner))
    ]
    for cp in metas:
        cp.start()

    total = spat[0]
    for k in range(1, 2 * RAD + 1):
        total = total + spat[k]
    tot = jnp.full((8, CB), total, F32)
    scale = 1.0 / (tot * tot)
    for q in range(CB // 8):
        row = iota((8, CB), 0) + 8 * q
        col = iota((8, CB), 1)
        main = row - col + RAD
        edge = jnp.where(row < 128, row - 128, row + 128) - col + RAD
        vm, ve = jnp.zeros((8, CB), F32), jnp.zeros((8, CB), F32)
        has_edge = 120 <= 8 * q < 136
        for k in range(2 * RAD + 1):
            vm = jnp.where(main == k, spat[k], vm)
            if has_edge:
                ve = jnp.where(edge == k, spat[k], ve)
        fbuf[q] = vm * scale
        fbuf[32 + q] = ve * scale
    h, l = split(fbuf[0:32].reshape(CB, CB))
    b0h[...], b0l[...] = h, l
    h, l = split(fbuf[32:64].reshape(CB, CB))
    b1h[...], b1l[...] = h, l
    rp[0] = jnp.zeros((TL, 8, CB), F32)
    rp[ND + 1] = jnp.zeros((TL, 8, CB), F32)

    def filter_chunk(g):
        def row_pass(t, carry):
            for p in range(ND):
                cols = slice(p * CB, (p + 1) * CB)
                acc = spat[0] * win[g, t, 2:10, cols]
                for k in range(1, 2 * RAD + 1):
                    acc = acc + spat[k] * win[g, t, 2 + k : 10 + k, cols]
                rp[p + 1, t] = acc
            return carry

        lax.fori_loop(0, TL, row_pass, 0)
        x = rp[1 : ND + 1].reshape(ND * TL * 8, CB)
        xh, xl = split(x)
        low = dot(xh, b0h[...]) + dot(xl, b0h[...]) + dot(xh, b0l[...])
        e = jnp.concatenate([rp[0:ND, :, :, 128:], rp[2 : ND + 2, :, :, :128]], axis=-1)
        eh, el = split(e.reshape(ND * TL * 8, CB))
        low = low + dot(eh, b1h[...]) + dot(el, b1h[...]) + dot(eh, b1l[...])
        low = low.reshape(ND, TL, 8, CB)
        for p in range(ND):
            sbuf[p, g] = win[g, :, 8:16, p * CB : (p + 1) * CB] - low[p]

    def bulk(g, k, into=rbuf):
        p = (d + k) % ND
        return pltpu.make_async_remote_copy(
            src_ref=sbuf.at[p, g],
            dst_ref=into.at[g, pl.ds(TL * d, TL)],
            send_sem=bulk_s.at[g, k],
            recv_sem=bulk_r.at[g, k],
            device_id=(p, s),
            device_id_type=MESH,
        )

    def send_chunk(g, into=rbuf):
        for k in range(1, ND):
            bulk(g, k, into).start()

    def keep(g, into=rbuf):
        return pltpu.make_async_copy(
            sbuf.at[d, g], into.at[g, pl.ds(TL * d, TL)], keep_sem.at[g]
        )

    def halo(down):
        src = stack.at[:, R - 8 : R, :] if down else stack.at[:, 0:8, :]
        dst = win.at[0, :, 0:8, :] if down else win.at[G - 1, :, 16:24, :]
        i = 0 if down else 1
        to = (s + 1) % NS if down else (s + NS - 1) % NS
        return pltpu.make_async_remote_copy(
            src_ref=src, dst_ref=dst, send_sem=halo_s.at[i], recv_sem=halo_r.at[i],
            device_id=(d, to), device_id_type=MESH,
        )

    def meta(k):
        return pltpu.make_async_remote_copy(
            src_ref=mloc, dst_ref=mall.at[d], send_sem=meta_s.at[k], recv_sem=meta_r.at[k],
            device_id=((d + k) % ND, s), device_id_type=MESH,
        )

    def wait_window(g):
        pltpu.make_async_copy(stack.at[:, 0:24, :], win.at[g], win_sem.at[g]).wait()

    wait_window(order[0])
    filter_chunk(order[0])
    pl.semaphore_wait(bar, ND - 1 + NS - 1)
    send_chunk(order[0])
    halo(True).start()
    halo(False).start()
    for cp in metas:
        cp.wait()
    for k in range(1, ND):
        meta(k).start()

    def interior(g, carry):
        wait_window(g)
        filter_chunk(g)
        send_chunk(g)
        return carry

    lax.fori_loop(2, G - 1, interior, 0)

    r_, c_ = iota((T, T), 0), iota((T, T), 1)
    r2, c2 = iota((T, 2 * T), 0), iota((T, 2 * T), 1) % T
    near = jnp.where(r_ == c_, 1.0, 0.0).astype(F32)
    far = jnp.where(r2 == c2, 1.0, 0.0).astype(F32)
    for k in range(5):
        near = near - jnp.where(r_ - c_ == k - 2, temp[0, k], 0.0)
        far = far - jnp.where(r2 - c2 == 8 * (k - 2), temp[1, k], 0.0)
    tt = jnp.dot(near, far, precision=lax.Precision.HIGHEST, preferred_element_type=F32)
    wh[...] = jnp.zeros(wh.shape, BF16)
    wl[...] = jnp.zeros(wl.shape, BF16)
    half = iota((8, 2 * T), 1) < T
    for i in range(ND):
        part = tt[8 * i : 8 * i + 8]
        base = jnp.concatenate([jnp.where(half, part, 0.0), jnp.where(half, 0.0, part)], axis=0)
        bh, bl = split(base)
        for p in range(ND):
            wh[i * 128 + 16 * p : i * 128 + 16 * p + 16, 128 * p : 128 * p + 128] = bh
            wl[i * 128 + 16 * p : i * 128 + 16 * p + 16, 128 * p : 128 * p + 128] = bl

    halo(True).wait()
    halo(False).wait()
    for g in (0, G - 1):
        window(g).wait()

    @pl.when(s == 0)
    def _():
        win[0, :, 0:8, :] = jnp.zeros((TL, 8, C), F32)

    @pl.when(s == NS - 1)
    def _():
        win[G - 1, :, 16:24, :] = jnp.zeros((TL, 8, C), F32)

    def edge_chunk(i, carry):
        filter_chunk((G - 1) * i)
        return carry

    lax.fori_loop(0, 2, edge_chunk, 0)

    mall[d] = mloc[...]
    for k in range(1, ND):
        meta(k).wait()
    cnt_t[...] = jnp.zeros(cnt_t.shape, F32)

    def block(p, carry):
        tile, row, count, owner = (mall[p, i] for i in range(4))
        jj = iota((CB, F), 0)
        inside = ((jj >> 7) == tile) & ((jj & 127) < count)
        m = jnp.where(inside, 1.0, 0.0).astype(BF16)
        xh, xl = split(sbuf[p].reshape(G * TL * 8, CB))
        g_ = (dot(xh, m) + dot(xl, m)).reshape(G, TL, 8, F)
        here = iota((G, 8, F), 0) * 8 + iota((G, 8, F), 1) == row.reshape(1, 1, F)
        picked = jnp.sum(jnp.where(here[:, None], g_, 0.0), axis=0)
        cf = count.astype(F32)
        mean = jnp.sum(picked, axis=1) / cf
        own = jnp.broadcast_to(owner.astype(F32), (F, F))
        own_t = own.T
        sub, lane = iota((F, F), 0), iota((F, F), 1)
        earlier = (own == own_t) & (sub < lane)
        slot = jnp.sum(jnp.where(earlier, 1.0, 0.0), axis=0, keepdims=True)
        onehot = jnp.where(own_t == lane.astype(F32), 1.0, 0.0)
        rows = jnp.concatenate(
            [
                jnp.where(slot == 0.0, mean, 0.0),
                jnp.where(slot == 1.0, mean, 0.0),
                jnp.where(iota((8, F), 0).astype(F32) == slot, cf, 0.0),
            ],
            axis=0,
        )
        got = jnp.dot(rows, onehot, precision=lax.Precision.HIGHEST, preferred_element_type=F32)
        out_t[pl.ds(pl.multiple_of(16 * p, 16), 16)] = got[0:16]
        cnt_t[pl.ds(pl.multiple_of(8 * p, 8), 8)] = got[16:24]
        return carry

    lax.fori_loop(0, ND, block, 0)
    obuf[...] = out_t[...].T
    cnt_o[...] = cnt_t[...].T

    def stage1(k):
        p = (d + k) % ND
        return pltpu.make_async_remote_copy(
            src_ref=obuf.at[pl.ds(pl.multiple_of(16 * p, 16), 16)], dst_ref=st1.at[d],
            send_sem=st1_s.at[k], recv_sem=st1_r.at[k],
            device_id=(p, s), device_id_type=MESH,
        )

    for k in range(1, ND):
        stage1(k).start()
    mine = pl.ds(pl.multiple_of(16 * d, 16), 16)
    st1[d] = obuf[mine]
    send_chunk(0)
    send_chunk(G - 1, gat_out)
    for g in range(G - 1):
        keep(g).start()
    keep(G - 1, gat_out).start()

    def result(g):
        return pltpu.make_async_copy(rbuf.at[g], gat_out.at[g], out_sem.at[g])

    def finish(g, carry):
        keep(g).wait()
        for k in range(1, ND):
            bulk(g, k).wait()
        filter_dates(rbuf.at[g], fbuf, rbuf.at[g], temp)
        result(g).start()
        return carry

    lax.fori_loop(1, G - 1, finish, 0)

    for k in range(1, ND):
        stage1(k).wait()
    ser = jnp.concatenate([st1[i] for i in range(ND)], axis=-1)
    sh, sl = split(ser)
    y = dot(sh, wh[...]) + dot(sl, wh[...]) + dot(sh, wl[...])
    cnt = cnt_o[mine]
    for i in range(NS):
        y2[i, :, 0 : 8 * F] = y[i : i + 1]
        y2[i, :, 8 * F : 9 * F] = cnt[i : i + 1]

    def stage2(k):
        o = (s + k) % NS
        return pltpu.make_async_remote_copy(
            src_ref=y2.at[o], dst_ref=z2.at[s],
            send_sem=st2_s.at[k], recv_sem=st2_r.at[k],
            device_id=(d, o), device_id_type=MESH,
        )

    for k in range(1, NS):
        stage2(k).start()
    z2[s] = y2[s]

    lax.fori_loop(0, 1, finish, 0)

    for k in range(1, NS):
        stage2(k).wait()
    for i in range(NS):
        zz[i : i + 1] = z2[i]
    z, cn = zz[:, 0 : 8 * F], zz[:, 8 * F : 9 * F]
    spread = jnp.where(
        iota((F, 8 * F), 0) == (iota((F, 8 * F), 1) // F) * 8 + (iota((F, 8 * F), 1) % F) // T, 1.0, 0.0
    ).astype(BF16)
    weight = dot(cn.astype(BF16), spread)
    part = jnp.sum(weight * z, axis=0, keepdims=True)
    acc = part[:, 0:F]
    for i in range(1, ND):
        acc = acc + part[:, i * F : (i + 1) * F]
    acc = acc + jnp.concatenate([acc[:, T:], acc[:, :T]], axis=1)
    asset = acc / jnp.sum(cn)
    for i in range(ND):
        cols = slice(i * F, (i + 1) * F)
        anom = jnp.where(weight[:, cols] > 0, z[:, cols] - asset, 0.0)
        xbuf[pl.ds(32 * i, NS, stride=2)] = anom
        xbuf[pl.ds(32 * i + 1, NS, stride=2)] = pltpu.roll(anom, T, 1)
    abuf[...] = xbuf[...].T[0:T]
    asbuf[...] = asset
    ends = [
        pltpu.make_async_copy(abuf, anom_out, fin_sem.at[0]),
        pltpu.make_async_copy(asbuf, asset_out, fin_sem.at[1]),
    ]
    for cp in ends:
        cp.start()
    for cp in ends:
        cp.wait()
    for g in range(G - 1):
        result(g).wait()
    keep(G - 1, gat_out).wait()
    for k in range(1, ND):
        bulk(G - 1, k, gat_out).wait()


def finish_kernel(gat, anom, asset, temp, res_out, anom_out, asset_out, xb, fb, in_sem, out_sem, fin_sem):
    def result(g):
        src = gat.at[g] if g < G - 1 else xb
        return pltpu.make_async_copy(src, res_out.at[:, 8 * g : 8 * g + 8, :], out_sem.at[g])

    last = pltpu.make_async_copy(gat.at[G - 1], xb, in_sem)
    last.start()
    for g in range(G - 1):
        result(g).start()
    ends = [
        pltpu.make_async_copy(anom, anom_out, fin_sem.at[0]),
        pltpu.make_async_copy(asset, asset_out, fin_sem.at[1]),
    ]
    for cp in ends:
        cp.start()
    last.wait()
    filter_dates(xb, fb, xb, temp)
    result(G - 1).start()
    for cp in ends:
        cp.wait()
    for g in range(G):
        result(g).wait()


def shards(stack, spatial_taps, temporal_taps, foot_tile, foot_row, foot_count, foot_owner):
    anywhere, smem = pl.BlockSpec(memory_space=pl.ANY), pl.BlockSpec(memory_space=pltpu.SMEM)
    hbm = pl.BlockSpec(memory_space=pltpu.HBM)
    vm, dma = pltpu.VMEM, pltpu.SemaphoreType.DMA
    scratch = [
        vm((G, TL, 24, C), F32), vm((ND + 2, TL, 8, CB), F32),
        vm((CB, CB), BF16), vm((CB, CB), BF16), vm((CB, CB), BF16), vm((CB, CB), BF16),
        vm((ND, G, TL, 8, CB), F32), vm((G, T, 8, CB), F32), vm((T, 8, CB), F32),
        vm((4, 1, F), I32), vm((ND, 4, 1, F), I32),
        vm((F, F), F32), vm((F, F), F32), vm((F, F), F32), vm((F, F), F32),
        vm((ND, NS, F), F32), vm((8 * F, 8 * F), BF16), vm((8 * F, 8 * F), BF16),
        vm((NS, 1, 9 * F), F32), vm((NS, 1, 9 * F), F32), vm((NS, 9 * F), F32),
        vm((2 * F, F), F32), vm((T, 2 * F), F32), vm((1, F), F32),
        dma((G,)), dma((4,)), dma((2,)), dma((2,)), dma((ND,)), dma((ND,)),
        dma((G, ND)), dma((G, ND)), dma((ND,)), dma((ND,)), dma((NS,)), dma((NS,)),
        dma((G,)), dma((G,)), dma((2,)),
    ]
    held = [
        pltpu.with_memory_space_constraint(a, pltpu.HBM)
        for a in (
            stack, spatial_taps, temporal_taps, foot_tile.reshape(1, F), foot_row.reshape(1, F),
            foot_count.reshape(1, F), foot_owner.reshape(1, F),
        )
    ]
    gathered, anomaly, asset = pl.pallas_call(
        kernel,
        out_shape=(
            jax.ShapeDtypeStruct((G, T, 8, CB), F32),
            jax.ShapeDtypeStruct((T, 2 * F), F32),
            jax.ShapeDtypeStruct((1, F), F32),
        ),
        in_specs=[hbm, smem, smem, anywhere, anywhere, anywhere, anywhere],
        out_specs=(anywhere, anywhere, anywhere),
        scratch_shapes=scratch,
        compiler_params=pltpu.CompilerParams(
            collective_id=0, has_side_effects=True, vmem_limit_bytes=44 << 20
        ),
        name="series",
    )(*held)
    residual, anomaly, asset = pl.pallas_call(
        finish_kernel,
        out_shape=(
            jax.ShapeDtypeStruct((T, R, CB), F32),
            jax.ShapeDtypeStruct((T, 2 * F), F32),
            jax.ShapeDtypeStruct((1, F), F32),
        ),
        in_specs=[anywhere, anywhere, anywhere, smem],
        out_specs=(hbm, hbm, hbm),
        scratch_shapes=[vm((T, 8, CB), F32), vm((T, 8, CB), F32), dma, dma((G,)), dma((2,))],
        compiler_params=pltpu.CompilerParams(vmem_limit_bytes=4 << 20),
        name="finish",
    )(gathered, anomaly, asset, temporal_taps)
    return residual, anomaly.T[None], asset[:, :T]


def solution(mesh):
    rows = P(("date", "strip"))
    return jax.shard_map(
        shards,
        mesh=mesh,
        in_specs=(P("date", "strip", None), P(), P(), rows, rows, rows, P(("date", "strip"), None)),
        out_specs=(P(None, "strip", "date"), P(("date", "strip"), None, None), P(("date", "strip"), None)),
        check_vma=False,
    )
```

```python
import functools
import jax
import jax.numpy as jnp
from jax import lax
from jax.experimental import pallas as pl
from jax.experimental.pallas import tpu as pltpu
from jax.sharding import PartitionSpec as P

MESH = pl.DeviceIdType.MESH
F32, BF16, I32 = jnp.float32, jnp.bfloat16, jnp.int32
ND, NS = 8, 16
T, TL = 64, 8
R, G = 64, 8
C, CB = 2048, 256
F = 128
RAD = 6
HT = 4


def dot(a, b):
    return jnp.dot(a, b, preferred_element_type=F32)


def split(x):
    hi = x.astype(BF16)
    return hi, (x - hi.astype(F32)).astype(BF16)


def iota(shape, dim):
    return lax.broadcasted_iota(I32, shape, dim)


def filter_dates(src, mid, dst, temp):
    ca = [-temp[0, k] for k in range(5)]
    cb = [-temp[1, k] for k in range(5)]
    ca[2], cb[2] = 1.0 + ca[2], 1.0 + cb[2]
    for a, b, coef, step in ((src, mid, ca, 1), (mid, dst, cb, 8)):
        for t in range(T):
            acc = coef[2] * a[t]
            for k in (0, 1, 3, 4):
                u = t + step * (k - 2)
                if 0 <= u < T:
                    acc = acc + coef[k] * a[u]
            b[t] = acc


def kernel(
    stack, spat, temp, ftile, frow, fcount, fowner,
    gat_out, anom_out, asset_out,
    win, rp, b0h, b0l, b1h, b1l, sbuf, rbuf, fbuf,
    mloc, mall, out_t, cnt_t, cnt_o, obuf, st1, wh, wl, y2, z2, zz, xbuf, abuf, asbuf,
    win_sem, ml_sem, halo_s, halo_r, meta_s, meta_r, bulk_s, bulk_r,
    st1_s, st1_r, st2_s, st2_r, keep_sem, out_sem, fin_sem, group_in, all_in,
):
    d = lax.axis_index("date")
    s = lax.axis_index("strip")

    bar = pltpu.get_barrier_semaphore()
    for k in range(1, ND):
        pl.semaphore_signal(bar, inc=1, device_id=((d + k) % ND, s), device_id_type=MESH)

    @pl.when(d == 0)
    def _():
        for k in range(1, NS):
            pl.semaphore_signal(bar, inc=1, device_id=(0, (s + k) % NS), device_id_type=MESH)

    def window(g):
        lo, hi = max(8 * g - 8, 0), min(8 * g + 16, R)
        at = lo - (8 * g - 8)
        return pltpu.make_async_copy(
            stack.at[:, lo:hi, :], win.at[g, :, at : at + hi - lo, :], win_sem.at[g]
        )

    def early(h):
        dates = slice(HT * h, HT * h + HT)
        return pltpu.make_async_copy(
            stack.at[dates, 0:24, :], win.at[order[0], dates], win_sem.at[G if h else order[0]]
        )

    order = [(i + 1) % G for i in range(G)]
    early(0).start()
    early(1).start()
    for g in order[1:]:
        window(g).start()
    metas = [
        pltpu.make_async_copy(ref, mloc.at[i], ml_sem.at[i])
        for i, ref in enumerate((ftile, frow, fcount, fowner))
    ]
    for cp in metas:
        cp.start()

    total = spat[0]
    for k in range(1, 2 * RAD + 1):
        total = total + spat[k]
    tot = jnp.full((8, CB), total, F32)
    scale = 1.0 / (tot * tot)
    for q in range(CB // 8):
        row = iota((8, CB), 0) + 8 * q
        col = iota((8, CB), 1)
        main = row - col + RAD
        edge = jnp.where(row < 128, row - 128, row + 128) - col + RAD
        vm, ve = jnp.zeros((8, CB), F32), jnp.zeros((8, CB), F32)
        has_edge = 120 <= 8 * q < 136
        for k in range(2 * RAD + 1):
            vm = jnp.where(main == k, spat[k], vm)
            if has_edge:
                ve = jnp.where(edge == k, spat[k], ve)
        fbuf[q] = vm * scale
        fbuf[32 + q] = ve * scale
    h, l = split(fbuf[0:32].reshape(CB, CB))
    b0h[...], b0l[...] = h, l
    h, l = split(fbuf[32:64].reshape(CB, CB))
    b1h[...], b1l[...] = h, l
    rp[0] = jnp.zeros((TL, 8, CB), F32)
    rp[ND + 1] = jnp.zeros((TL, 8, CB), F32)

    def filter_chunk(g, first=None):
        t0, nt = (0, TL) if first is None else (first, HT)
        dates = slice(t0, t0 + nt)

        def row_pass(t, carry):
            for p in range(ND):
                cols = slice(p * CB, (p + 1) * CB)
                acc = spat[0] * win[g, t, 2:10, cols]
                for k in range(1, 2 * RAD + 1):
                    acc = acc + spat[k] * win[g, t, 2 + k : 10 + k, cols]
                rp[p + 1, t] = acc
            return carry

        lax.fori_loop(t0, t0 + nt, row_pass, 0)
        x = rp[1 : ND + 1, dates].reshape(ND * nt * 8, CB)
        xh, xl = split(x)
        low = dot(xh, b0h[...]) + dot(xl, b0h[...]) + dot(xh, b0l[...])
        e = jnp.concatenate([rp[0:ND, dates, :, 128:], rp[2 : ND + 2, dates, :, :128]], axis=-1)
        eh, el = split(e.reshape(ND * nt * 8, CB))
        low = low + dot(eh, b1h[...]) + dot(el, b1h[...]) + dot(eh, b1l[...])
        low = low.reshape(ND, nt, 8, CB)
        for p in range(ND):
            sbuf[p, g, dates] = win[g, dates, 8:16, p * CB : (p + 1) * CB] - low[p]

    def bulk(g, k, into=rbuf):
        p = (d + k) % ND
        return pltpu.make_async_remote_copy(
            src_ref=sbuf.at[p, g],
            dst_ref=into.at[g, pl.ds(TL * d, TL)],
            send_sem=bulk_s.at[g, k],
            recv_sem=bulk_r.at[g, k],
            device_id=(p, s),
            device_id_type=MESH,
        )

    def half(h, k):
        g, p = order[0], (d + k) % ND
        return pltpu.make_async_remote_copy(
            src_ref=sbuf.at[p, g, pl.ds(HT * h, HT)],
            dst_ref=rbuf.at[g, pl.ds(TL * d + HT * h, HT)],
            send_sem=bulk_s.at[g if h else G, k],
            recv_sem=bulk_r.at[g if h else G, k],
            device_id=(p, s),
            device_id_type=MESH,
        )

    def send_half(h):
        for k in range(1, ND):
            half(h, k).start()

    def send_chunk(g, into=rbuf):
        for k in range(1, ND):
            bulk(g, k, into).start()

    def keep(g, into=rbuf):
        return pltpu.make_async_copy(
            sbuf.at[d, g], into.at[g, pl.ds(TL * d, TL)], keep_sem.at[g]
        )

    def halo(down):
        src = stack.at[:, R - 8 : R, :] if down else stack.at[:, 0:8, :]
        dst = win.at[0, :, 0:8, :] if down else win.at[G - 1, :, 16:24, :]
        i = 0 if down else 1
        to = (s + 1) % NS if down else (s + NS - 1) % NS
        return pltpu.make_async_remote_copy(
            src_ref=src, dst_ref=dst, send_sem=halo_s.at[i], recv_sem=halo_r.at[i],
            device_id=(d, to), device_id_type=MESH,
        )

    def meta(k):
        return pltpu.make_async_remote_copy(
            src_ref=mloc, dst_ref=mall.at[d], send_sem=meta_s.at[k], recv_sem=meta_r.at[k],
            device_id=((d + k) % ND, s), device_id_type=MESH,
        )

    def wait_window(g):
        pltpu.make_async_copy(stack.at[:, 0:24, :], win.at[g], win_sem.at[g]).wait()

    early(0).wait()
    filter_chunk(order[0], 0)
    pl.semaphore_wait(bar, jnp.where(d == 0, ND - 1 + NS - 1, ND - 1))
    send_half(0)
    early(1).wait()
    filter_chunk(order[0], HT)
    send_half(1)
    for cp in metas:
        cp.wait()
    for k in range(1, ND):
        meta(k).start()

    def interior(g, carry):
        wait_window(g)
        filter_chunk(g)
        send_chunk(g)
        return carry

    lax.fori_loop(2, 3, interior, 0)

    @pl.when(d == 0)
    def _():
        for k in range(1, NS):
            pl.semaphore_signal(group_in, inc=1, device_id=(0, (s + k) % NS), device_id_type=MESH)
        pl.semaphore_wait(group_in, NS - 1)
        for k in range(1, ND):
            pl.semaphore_signal(all_in, inc=1, device_id=(k, s), device_id_type=MESH)

    @pl.when(d != 0)
    def _():
        pl.semaphore_wait(all_in, 1)

    halo(True).start()
    halo(False).start()

    lax.fori_loop(3, G - 1, interior, 0)

    r_, c_ = iota((T, T), 0), iota((T, T), 1)
    r2, c2 = iota((T, 2 * T), 0), iota((T, 2 * T), 1) % T
    near = jnp.where(r_ == c_, 1.0, 0.0).astype(F32)
    far = jnp.where(r2 == c2, 1.0, 0.0).astype(F32)
    for k in range(5):
        near = near - jnp.where(r_ - c_ == k - 2, temp[0, k], 0.0)
        far = far - jnp.where(r2 - c2 == 8 * (k - 2), temp[1, k], 0.0)
    tt = jnp.dot(near, far, precision=lax.Precision.HIGHEST, preferred_element_type=F32)
    wh[...] = jnp.zeros(wh.shape, BF16)
    wl[...] = jnp.zeros(wl.shape, BF16)
    left = iota((8, 2 * T), 1) < T
    for i in range(ND):
        part = tt[8 * i : 8 * i + 8]
        base = jnp.concatenate([jnp.where(left, part, 0.0), jnp.where(left, 0.0, part)], axis=0)
        bh, bl = split(base)
        for p in range(ND):
            wh[i * 128 + 16 * p : i * 128 + 16 * p + 16, 128 * p : 128 * p + 128] = bh
            wl[i * 128 + 16 * p : i * 128 + 16 * p + 16, 128 * p : 128 * p + 128] = bl

    halo(True).wait()
    halo(False).wait()
    for g in (0, G - 1):
        window(g).wait()

    @pl.when(s == 0)
    def _():
        win[0, :, 0:8, :] = jnp.zeros((TL, 8, C), F32)

    @pl.when(s == NS - 1)
    def _():
        win[G - 1, :, 16:24, :] = jnp.zeros((TL, 8, C), F32)

    def edge_chunk(i, carry):
        filter_chunk((G - 1) * i)
        return carry

    lax.fori_loop(0, 2, edge_chunk, 0)

    mall[d] = mloc[...]
    for k in range(1, ND):
        meta(k).wait()
    cnt_t[...] = jnp.zeros(cnt_t.shape, F32)

    def block(p, carry):
        tile, row, count, owner = (mall[p, i] for i in range(4))
        jj = iota((CB, F), 0)
        inside = ((jj >> 7) == tile) & ((jj & 127) < count)
        m = jnp.where(inside, 1.0, 0.0).astype(BF16)
        xh, xl = split(sbuf[p].reshape(G * TL * 8, CB))
        g_ = (dot(xh, m) + dot(xl, m)).reshape(G, TL, 8, F)
        here = iota((G, 8, F), 0) * 8 + iota((G, 8, F), 1) == row.reshape(1, 1, F)
        picked = jnp.sum(jnp.where(here[:, None], g_, 0.0), axis=0)
        cf = count.astype(F32)
        mean = jnp.sum(picked, axis=1) / cf
        own = jnp.broadcast_to(owner.astype(F32), (F, F))
        own_t = own.T
        sub, lane = iota((F, F), 0), iota((F, F), 1)
        earlier = (own == own_t) & (sub < lane)
        slot = jnp.sum(jnp.where(earlier, 1.0, 0.0), axis=0, keepdims=True)
        onehot = jnp.where(own_t == lane.astype(F32), 1.0, 0.0)
        rows = jnp.concatenate(
            [
                jnp.where(slot == 0.0, mean, 0.0),
                jnp.where(slot == 1.0, mean, 0.0),
                jnp.where(iota((8, F), 0).astype(F32) == slot, cf, 0.0),
            ],
            axis=0,
        )
        got = jnp.dot(rows, onehot, precision=lax.Precision.HIGHEST, preferred_element_type=F32)
        out_t[pl.ds(pl.multiple_of(16 * p, 16), 16)] = got[0:16]
        cnt_t[pl.ds(pl.multiple_of(8 * p, 8), 8)] = got[16:24]
        return carry

    lax.fori_loop(0, ND, block, 0)
    obuf[...] = out_t[...].T
    cnt_o[...] = cnt_t[...].T

    def stage1(k):
        p = (d + k) % ND
        return pltpu.make_async_remote_copy(
            src_ref=obuf.at[pl.ds(pl.multiple_of(16 * p, 16), 16)], dst_ref=st1.at[d],
            send_sem=st1_s.at[k], recv_sem=st1_r.at[k],
            device_id=(p, s), device_id_type=MESH,
        )

    for k in range(1, ND):
        stage1(k).start()
    mine = pl.ds(pl.multiple_of(16 * d, 16), 16)
    st1[d] = obuf[mine]
    send_chunk(0)
    send_chunk(G - 1, gat_out)
    for g in range(G - 1):
        keep(g).start()
    keep(G - 1, gat_out).start()

    def result(g):
        return pltpu.make_async_copy(rbuf.at[g], gat_out.at[g], out_sem.at[g])

    def finish(g, carry):
        keep(g).wait()
        for k in range(1, ND):
            bulk(g, k).wait()
        complete(g)
        return carry

    def complete(g):
        filter_dates(rbuf.at[g], fbuf, rbuf.at[g], temp)
        result(g).start()

    keep(order[0]).wait()
    for k in range(1, ND):
        half(0, k).wait()
        half(1, k).wait()
    complete(order[0])
    lax.fori_loop(2, G - 1, finish, 0)

    for k in range(1, ND):
        stage1(k).wait()
    ser = jnp.concatenate([st1[i] for i in range(ND)], axis=-1)
    sh, sl = split(ser)
    y = dot(sh, wh[...]) + dot(sl, wh[...]) + dot(sh, wl[...])
    cnt = cnt_o[mine]
    for i in range(NS):
        y2[i, :, 0 : 8 * F] = y[i : i + 1]
        y2[i, :, 8 * F : 9 * F] = cnt[i : i + 1]

    def stage2(k):
        o = (s + k) % NS
        return pltpu.make_async_remote_copy(
            src_ref=y2.at[o], dst_ref=z2.at[s],
            send_sem=st2_s.at[k], recv_sem=st2_r.at[k],
            device_id=(d, o), device_id_type=MESH,
        )

    for k in range(1, NS):
        stage2(k).start()
    z2[s] = y2[s]

    lax.fori_loop(0, 1, finish, 0)

    for k in range(1, NS):
        stage2(k).wait()
    for i in range(NS):
        zz[i : i + 1] = z2[i]
    z, cn = zz[:, 0 : 8 * F], zz[:, 8 * F : 9 * F]
    spread = jnp.where(
        iota((F, 8 * F), 0) == (iota((F, 8 * F), 1) // F) * 8 + (iota((F, 8 * F), 1) % F) // T, 1.0, 0.0
    ).astype(BF16)
    weight = dot(cn.astype(BF16), spread)
    part = jnp.sum(weight * z, axis=0, keepdims=True)
    acc = part[:, 0:F]
    for i in range(1, ND):
        acc = acc + part[:, i * F : (i + 1) * F]
    acc = acc + jnp.concatenate([acc[:, T:], acc[:, :T]], axis=1)
    asset = acc / jnp.sum(cn)
    for i in range(ND):
        cols = slice(i * F, (i + 1) * F)
        anom = jnp.where(weight[:, cols] > 0, z[:, cols] - asset, 0.0)
        xbuf[pl.ds(32 * i, NS, stride=2)] = anom
        xbuf[pl.ds(32 * i + 1, NS, stride=2)] = pltpu.roll(anom, T, 1)
    abuf[...] = xbuf[...].T[0:T]
    asbuf[...] = asset
    ends = [
        pltpu.make_async_copy(abuf, anom_out, fin_sem.at[0]),
        pltpu.make_async_copy(asbuf, asset_out, fin_sem.at[1]),
    ]
    for cp in ends:
        cp.start()
    for cp in ends:
        cp.wait()
    for g in range(G - 1):
        result(g).wait()
    keep(G - 1, gat_out).wait()
    for k in range(1, ND):
        bulk(G - 1, k, gat_out).wait()


def finish_kernel(gat, anom, asset, temp, res_out, anom_out, asset_out, xb, fb, in_sem, out_sem, fin_sem):
    def result(g):
        src = gat.at[g] if g < G - 1 else xb
        return pltpu.make_async_copy(src, res_out.at[:, 8 * g : 8 * g + 8, :], out_sem.at[g])

    last = pltpu.make_async_copy(gat.at[G - 1], xb, in_sem)
    last.start()
    for g in range(G - 1):
        result(g).start()
    ends = [
        pltpu.make_async_copy(anom, anom_out, fin_sem.at[0]),
        pltpu.make_async_copy(asset, asset_out, fin_sem.at[1]),
    ]
    for cp in ends:
        cp.start()
    last.wait()
    filter_dates(xb, fb, xb, temp)
    result(G - 1).start()
    for cp in ends:
        cp.wait()
    for g in range(G):
        result(g).wait()


def shards(stack, spatial_taps, temporal_taps, foot_tile, foot_row, foot_count, foot_owner):
    anywhere, smem = pl.BlockSpec(memory_space=pl.ANY), pl.BlockSpec(memory_space=pltpu.SMEM)
    hbm = pl.BlockSpec(memory_space=pltpu.HBM)
    vm, dma = pltpu.VMEM, pltpu.SemaphoreType.DMA
    scratch = [
        vm((G, TL, 24, C), F32), vm((ND + 2, TL, 8, CB), F32),
        vm((CB, CB), BF16), vm((CB, CB), BF16), vm((CB, CB), BF16), vm((CB, CB), BF16),
        vm((ND, G, TL, 8, CB), F32), vm((G, T, 8, CB), F32), vm((T, 8, CB), F32),
        vm((4, 1, F), I32), vm((ND, 4, 1, F), I32),
        vm((F, F), F32), vm((F, F), F32), vm((F, F), F32), vm((F, F), F32),
        vm((ND, NS, F), F32), vm((8 * F, 8 * F), BF16), vm((8 * F, 8 * F), BF16),
        vm((NS, 1, 9 * F), F32), vm((NS, 1, 9 * F), F32), vm((NS, 9 * F), F32),
        vm((2 * F, F), F32), vm((T, 2 * F), F32), vm((1, F), F32),
        dma((G + 1,)), dma((4,)), dma((2,)), dma((2,)), dma((ND,)), dma((ND,)),
        dma((G + 1, ND)), dma((G + 1, ND)), dma((ND,)), dma((ND,)), dma((NS,)), dma((NS,)),
        dma((G,)), dma((G,)), dma((2,)),
        pltpu.SemaphoreType.REGULAR, pltpu.SemaphoreType.REGULAR,
    ]
    held = [
        pltpu.with_memory_space_constraint(a, pltpu.HBM)
        for a in (
            stack, spatial_taps, temporal_taps, foot_tile.reshape(1, F), foot_row.reshape(1, F),
            foot_count.reshape(1, F), foot_owner.reshape(1, F),
        )
    ]
    gathered, anomaly, asset = pl.pallas_call(
        kernel,
        out_shape=(
            jax.ShapeDtypeStruct((G, T, 8, CB), F32),
            jax.ShapeDtypeStruct((T, 2 * F), F32),
            jax.ShapeDtypeStruct((1, F), F32),
        ),
        in_specs=[hbm, smem, smem, anywhere, anywhere, anywhere, anywhere],
        out_specs=(anywhere, anywhere, anywhere),
        scratch_shapes=scratch,
        compiler_params=pltpu.CompilerParams(
            collective_id=0, has_side_effects=True, vmem_limit_bytes=44 << 20
        ),
        name="series",
    )(*held)
    residual, anomaly, asset = pl.pallas_call(
        finish_kernel,
        out_shape=(
            jax.ShapeDtypeStruct((T, R, CB), F32),
            jax.ShapeDtypeStruct((T, 2 * F), F32),
            jax.ShapeDtypeStruct((1, F), F32),
        ),
        in_specs=[anywhere, anywhere, anywhere, smem],
        out_specs=(hbm, hbm, hbm),
        scratch_shapes=[vm((T, 8, CB), F32), vm((T, 8, CB), F32), dma, dma((G,)), dma((2,))],
        compiler_params=pltpu.CompilerParams(vmem_limit_bytes=4 << 20),
        name="finish",
    )(gathered, anomaly, asset, temporal_taps)
    return residual, anomaly.T[None], asset[:, :T]


def solution(mesh):
    rows = P(("date", "strip"))
    return jax.shard_map(
        shards,
        mesh=mesh,
        in_specs=(P("date", "strip", None), P(), P(), rows, rows, rows, P(("date", "strip"), None)),
        out_specs=(P(None, "strip", "date"), P(("date", "strip"), None, None), P(("date", "strip"), None)),
        check_vma=False,
    )
```

```python
import functools
import jax
import jax.numpy as jnp
from jax import lax
from jax.experimental import pallas as pl
from jax.experimental.pallas import tpu as pltpu
from jax.sharding import PartitionSpec as P

MESH = pl.DeviceIdType.MESH
F32, BF16, I32 = jnp.float32, jnp.bfloat16, jnp.int32
ND, NS = 8, 16
T, TL = 64, 8
R, G = 64, 8
C, CB = 2048, 256
F = 128
RAD = 6
HT = 4


def dot(a, b):
    return jnp.dot(a, b, preferred_element_type=F32)


def split(x):
    hi = x.astype(BF16)
    return hi, (x - hi.astype(F32)).astype(BF16)


def iota(shape, dim):
    return lax.broadcasted_iota(I32, shape, dim)


def filter_dates(src, mid, dst, temp):
    ca = [-temp[0, k] for k in range(5)]
    cb = [-temp[1, k] for k in range(5)]
    ca[2], cb[2] = 1.0 + ca[2], 1.0 + cb[2]
    for a, b, coef, step in ((src, mid, ca, 1), (mid, dst, cb, 8)):
        for t in range(T):
            acc = coef[2] * a[t]
            for k in (0, 1, 3, 4):
                u = t + step * (k - 2)
                if 0 <= u < T:
                    acc = acc + coef[k] * a[u]
            b[t] = acc


def kernel(
    stack, spat_in, temp_in, ftile, frow, fcount, fowner,
    gat_out, anom_out, asset_out,
    spat, temp, win, rp, b0h, b0l, b1h, b1l, sbuf, rbuf, fbuf,
    mloc, mall, out_t, cnt_t, cnt_o, obuf, st1, wh, wl, y2, z2, zz, xbuf, abuf, asbuf,
    tap_sem, win_sem, ml_sem, halo_s, halo_r, meta_s, meta_r, bulk_s, bulk_r,
    st1_s, st1_r, st2_s, st2_r, keep_sem, out_sem, fin_sem, group_in, all_in,
):
    d = lax.axis_index("date")
    s = lax.axis_index("strip")

    bar = pltpu.get_barrier_semaphore()
    for k in range(1, ND):
        pl.semaphore_signal(bar, inc=1, device_id=((d + k) % ND, s), device_id_type=MESH)

    @pl.when(d == 0)
    def _():
        for k in range(1, NS):
            pl.semaphore_signal(bar, inc=1, device_id=(0, (s + k) % NS), device_id_type=MESH)

    def window(g):
        lo, hi = max(8 * g - 8, 0), min(8 * g + 16, R)
        at = lo - (8 * g - 8)
        return pltpu.make_async_copy(
            stack.at[:, lo:hi, :], win.at[g, :, at : at + hi - lo, :], win_sem.at[g]
        )

    def early(h):
        dates = slice(HT * h, HT * h + HT)
        return pltpu.make_async_copy(
            stack.at[dates, 0:24, :], win.at[order[0], dates], win_sem.at[G if h else order[0]]
        )

    order = [(i + 1) % G for i in range(G)]
    taps = [
        pltpu.make_async_copy(spat_in, spat, tap_sem.at[0]),
        pltpu.make_async_copy(temp_in, temp, tap_sem.at[1]),
    ]
    for cp in taps:
        cp.start()
    early(0).start()
    early(1).start()
    for g in order[1:]:
        window(g).start()
    metas = [
        pltpu.make_async_copy(ref, mloc.at[i], ml_sem.at[i])
        for i, ref in enumerate((ftile, frow, fcount, fowner))
    ]
    for cp in metas:
        cp.start()

    for cp in taps:
        cp.wait()

    total = spat[0]
    for k in range(1, 2 * RAD + 1):
        total = total + spat[k]
    tot = jnp.full((8, CB), total, F32)
    scale = 1.0 / (tot * tot)
    for q in range(CB // 8):
        row = iota((8, CB), 0) + 8 * q
        col = iota((8, CB), 1)
        main = row - col + RAD
        edge = jnp.where(row < 128, row - 128, row + 128) - col + RAD
        vm, ve = jnp.zeros((8, CB), F32), jnp.zeros((8, CB), F32)
        has_edge = 120 <= 8 * q < 136
        for k in range(2 * RAD + 1):
            vm = jnp.where(main == k, spat[k], vm)
            if has_edge:
                ve = jnp.where(edge == k, spat[k], ve)
        fbuf[q] = vm * scale
        fbuf[32 + q] = ve * scale
    h, l = split(fbuf[0:32].reshape(CB, CB))
    b0h[...], b0l[...] = h, l
    h, l = split(fbuf[32:64].reshape(CB, CB))
    b1h[...], b1l[...] = h, l
    rp[0] = jnp.zeros((TL, 8, CB), F32)
    rp[ND + 1] = jnp.zeros((TL, 8, CB), F32)

    def filter_chunk(g, first=None):
        t0, nt = (0, TL) if first is None else (first, HT)
        dates = slice(t0, t0 + nt)

        def row_pass(t, carry):
            for p in range(ND):
                cols = slice(p * CB, (p + 1) * CB)
                acc = spat[0] * win[g, t, 2:10, cols]
                for k in range(1, 2 * RAD + 1):
                    acc = acc + spat[k] * win[g, t, 2 + k : 10 + k, cols]
                rp[p + 1, t] = acc
            return carry

        lax.fori_loop(t0, t0 + nt, row_pass, 0)
        x = rp[1 : ND + 1, dates].reshape(ND * nt * 8, CB)
        xh, xl = split(x)
        low = dot(xh, b0h[...]) + dot(xl, b0h[...]) + dot(xh, b0l[...])
        e = jnp.concatenate([rp[0:ND, dates, :, 128:], rp[2 : ND + 2, dates, :, :128]], axis=-1)
        eh, el = split(e.reshape(ND * nt * 8, CB))
        low = low + dot(eh, b1h[...]) + dot(el, b1h[...]) + dot(eh, b1l[...])
        low = low.reshape(ND, nt, 8, CB)
        for p in range(ND):
            sbuf[p, g, dates] = win[g, dates, 8:16, p * CB : (p + 1) * CB] - low[p]

    def bulk(g, k, into=rbuf):
        p = (d + k) % ND
        return pltpu.make_async_remote_copy(
            src_ref=sbuf.at[p, g],
            dst_ref=into.at[g, pl.ds(TL * d, TL)],
            send_sem=bulk_s.at[g, k],
            recv_sem=bulk_r.at[g, k],
            device_id=(p, s),
            device_id_type=MESH,
        )

    def half(h, k):
        g, p = order[0], (d + k) % ND
        return pltpu.make_async_remote_copy(
            src_ref=sbuf.at[p, g, pl.ds(HT * h, HT)],
            dst_ref=rbuf.at[g, pl.ds(TL * d + HT * h, HT)],
            send_sem=bulk_s.at[g if h else G, k],
            recv_sem=bulk_r.at[g if h else G, k],
            device_id=(p, s),
            device_id_type=MESH,
        )

    def send_half(h):
        for k in range(1, ND):
            half(h, k).start()

    def send_chunk(g, into=rbuf):
        for k in range(1, ND):
            bulk(g, k, into).start()

    def keep(g, into=rbuf):
        return pltpu.make_async_copy(
            sbuf.at[d, g], into.at[g, pl.ds(TL * d, TL)], keep_sem.at[g]
        )

    def halo(down):
        src = stack.at[:, R - 8 : R, :] if down else stack.at[:, 0:8, :]
        dst = win.at[0, :, 0:8, :] if down else win.at[G - 1, :, 16:24, :]
        i = 0 if down else 1
        to = (s + 1) % NS if down else (s + NS - 1) % NS
        return pltpu.make_async_remote_copy(
            src_ref=src, dst_ref=dst, send_sem=halo_s.at[i], recv_sem=halo_r.at[i],
            device_id=(d, to), device_id_type=MESH,
        )

    def meta(k):
        return pltpu.make_async_remote_copy(
            src_ref=mloc, dst_ref=mall.at[d], send_sem=meta_s.at[k], recv_sem=meta_r.at[k],
            device_id=((d + k) % ND, s), device_id_type=MESH,
        )

    def wait_window(g):
        pltpu.make_async_copy(stack.at[:, 0:24, :], win.at[g], win_sem.at[g]).wait()

    early(0).wait()
    filter_chunk(order[0], 0)
    pl.semaphore_wait(bar, jnp.where(d == 0, ND - 1 + NS - 1, ND - 1))
    send_half(0)

    @pl.when(d == 0)
    def _():
        for k in range(1, NS):
            pl.semaphore_signal(group_in, inc=1, device_id=(0, (s + k) % NS), device_id_type=MESH)

    early(1).wait()
    filter_chunk(order[0], HT)
    send_half(1)
    for cp in metas:
        cp.wait()
    for k in range(1, ND):
        meta(k).start()

    def interior(g, carry):
        wait_window(g)
        filter_chunk(g)
        send_chunk(g)
        return carry

    lax.fori_loop(2, 3, interior, 0)

    @pl.when(d == 0)
    def _():
        pl.semaphore_wait(group_in, NS - 1)
        for k in range(1, ND):
            pl.semaphore_signal(all_in, inc=1, device_id=(k, s), device_id_type=MESH)

    lax.fori_loop(3, 4, interior, 0)

    @pl.when(d != 0)
    def _():
        pl.semaphore_wait(all_in, 1)

    halo(True).start()
    halo(False).start()

    lax.fori_loop(4, G - 1, interior, 0)

    r_, c_ = iota((T, T), 0), iota((T, T), 1)
    r2, c2 = iota((T, 2 * T), 0), iota((T, 2 * T), 1) % T
    near = jnp.where(r_ == c_, 1.0, 0.0).astype(F32)
    far = jnp.where(r2 == c2, 1.0, 0.0).astype(F32)
    for k in range(5):
        near = near - jnp.where(r_ - c_ == k - 2, temp[0, k], 0.0)
        far = far - jnp.where(r2 - c2 == 8 * (k - 2), temp[1, k], 0.0)
    tt = jnp.dot(near, far, precision=lax.Precision.HIGHEST, preferred_element_type=F32)
    wh[...] = jnp.zeros(wh.shape, BF16)
    wl[...] = jnp.zeros(wl.shape, BF16)
    left = iota((8, 2 * T), 1) < T
    for i in range(ND):
        part = tt[8 * i : 8 * i + 8]
        base = jnp.concatenate([jnp.where(left, part, 0.0), jnp.where(left, 0.0, part)], axis=0)
        bh, bl = split(base)
        for p in range(ND):
            wh[i * 128 + 16 * p : i * 128 + 16 * p + 16, 128 * p : 128 * p + 128] = bh
            wl[i * 128 + 16 * p : i * 128 + 16 * p + 16, 128 * p : 128 * p + 128] = bl

    halo(True).wait()
    halo(False).wait()
    for g in (0, G - 1):
        window(g).wait()

    @pl.when(s == 0)
    def _():
        win[0, :, 0:8, :] = jnp.zeros((TL, 8, C), F32)

    @pl.when(s == NS - 1)
    def _():
        win[G - 1, :, 16:24, :] = jnp.zeros((TL, 8, C), F32)

    def edge_chunk(i, carry):
        filter_chunk((G - 1) * i)
        return carry

    lax.fori_loop(0, 2, edge_chunk, 0)

    mall[d] = mloc[...]
    for k in range(1, ND):
        meta(k).wait()
    cnt_t[...] = jnp.zeros(cnt_t.shape, F32)

    def block(p, carry):
        tile, row, count, owner = (mall[p, i] for i in range(4))
        jj = iota((CB, F), 0)
        inside = ((jj >> 7) == tile) & ((jj & 127) < count)
        m = jnp.where(inside, 1.0, 0.0).astype(BF16)
        xh, xl = split(sbuf[p].reshape(G * TL * 8, CB))
        g_ = (dot(xh, m) + dot(xl, m)).reshape(G, TL, 8, F)
        here = iota((G, 8, F), 0) * 8 + iota((G, 8, F), 1) == row.reshape(1, 1, F)
        picked = jnp.sum(jnp.where(here[:, None], g_, 0.0), axis=0)
        cf = count.astype(F32)
        mean = jnp.sum(picked, axis=1) / cf
        own = jnp.broadcast_to(owner.astype(F32), (F, F))
        own_t = own.T
        sub, lane = iota((F, F), 0), iota((F, F), 1)
        earlier = (own == own_t) & (sub < lane)
        slot = jnp.sum(jnp.where(earlier, 1.0, 0.0), axis=0, keepdims=True)
        onehot = jnp.where(own_t == lane.astype(F32), 1.0, 0.0)
        rows = jnp.concatenate(
            [
                jnp.where(slot == 0.0, mean, 0.0),
                jnp.where(slot == 1.0, mean, 0.0),
                jnp.where(iota((8, F), 0).astype(F32) == slot, cf, 0.0),
            ],
            axis=0,
        )
        got = jnp.dot(rows, onehot, precision=lax.Precision.HIGHEST, preferred_element_type=F32)
        out_t[pl.ds(pl.multiple_of(16 * p, 16), 16)] = got[0:16]
        cnt_t[pl.ds(pl.multiple_of(8 * p, 8), 8)] = got[16:24]
        return carry

    lax.fori_loop(0, ND, block, 0)
    obuf[...] = out_t[...].T
    cnt_o[...] = cnt_t[...].T

    def stage1(k):
        p = (d + k) % ND
        return pltpu.make_async_remote_copy(
            src_ref=obuf.at[pl.ds(pl.multiple_of(16 * p, 16), 16)], dst_ref=st1.at[d],
            send_sem=st1_s.at[k], recv_sem=st1_r.at[k],
            device_id=(p, s), device_id_type=MESH,
        )

    for k in range(1, ND):
        stage1(k).start()
    mine = pl.ds(pl.multiple_of(16 * d, 16), 16)
    st1[d] = obuf[mine]
    send_chunk(0)
    send_chunk(G - 1, gat_out)
    for g in range(G - 1):
        keep(g).start()
    keep(G - 1, gat_out).start()

    def result(g):
        return pltpu.make_async_copy(rbuf.at[g], gat_out.at[g], out_sem.at[g])

    def finish(g, carry):
        keep(g).wait()
        for k in range(1, ND):
            bulk(g, k).wait()
        complete(g)
        return carry

    def complete(g):
        filter_dates(rbuf.at[g], fbuf, rbuf.at[g], temp)
        result(g).start()

    keep(order[0]).wait()
    for k in range(1, ND):
        half(0, k).wait()
        half(1, k).wait()
    complete(order[0])
    lax.fori_loop(2, G - 1, finish, 0)

    for k in range(1, ND):
        stage1(k).wait()
    ser = jnp.concatenate([st1[i] for i in range(ND)], axis=-1)
    sh, sl = split(ser)
    y = dot(sh, wh[...]) + dot(sl, wh[...]) + dot(sh, wl[...])
    cnt = cnt_o[mine]
    for i in range(NS):
        y2[i, :, 0 : 8 * F] = y[i : i + 1]
        y2[i, :, 8 * F : 9 * F] = cnt[i : i + 1]

    def stage2(k):
        o = (s + k) % NS
        return pltpu.make_async_remote_copy(
            src_ref=y2.at[o], dst_ref=z2.at[s],
            send_sem=st2_s.at[k], recv_sem=st2_r.at[k],
            device_id=(d, o), device_id_type=MESH,
        )

    for k in range(1, NS):
        stage2(k).start()
    z2[s] = y2[s]

    lax.fori_loop(0, 1, finish, 0)

    for k in range(1, NS):
        stage2(k).wait()
    for i in range(NS):
        zz[i : i + 1] = z2[i]
    z, cn = zz[:, 0 : 8 * F], zz[:, 8 * F : 9 * F]
    spread = jnp.where(
        iota((F, 8 * F), 0) == (iota((F, 8 * F), 1) // F) * 8 + (iota((F, 8 * F), 1) % F) // T, 1.0, 0.0
    ).astype(BF16)
    weight = dot(cn.astype(BF16), spread)
    part = jnp.sum(weight * z, axis=0, keepdims=True)
    acc = part[:, 0:F]
    for i in range(1, ND):
        acc = acc + part[:, i * F : (i + 1) * F]
    acc = acc + jnp.concatenate([acc[:, T:], acc[:, :T]], axis=1)
    asset = acc / jnp.sum(cn)
    for i in range(ND):
        cols = slice(i * F, (i + 1) * F)
        anom = jnp.where(weight[:, cols] > 0, z[:, cols] - asset, 0.0)
        xbuf[pl.ds(32 * i, NS, stride=2)] = anom
        xbuf[pl.ds(32 * i + 1, NS, stride=2)] = pltpu.roll(anom, T, 1)
    abuf[...] = xbuf[...].T[0:T]
    asbuf[...] = asset
    ends = [
        pltpu.make_async_copy(abuf, anom_out, fin_sem.at[0]),
        pltpu.make_async_copy(asbuf, asset_out, fin_sem.at[1]),
    ]
    for cp in ends:
        cp.start()
    for cp in ends:
        cp.wait()
    for g in range(G - 1):
        result(g).wait()
    keep(G - 1, gat_out).wait()
    for k in range(1, ND):
        bulk(G - 1, k, gat_out).wait()


def finish_kernel(
    gat, anom, asset, temp_in, res_out, anom_out, asset_out, temp, xb, fb, in_sem, tap_sem, out_sem, fin_sem
):
    taps = pltpu.make_async_copy(temp_in, temp, tap_sem)
    taps.start()

    def result(g):
        src = gat.at[g] if g < G - 1 else xb
        return pltpu.make_async_copy(src, res_out.at[:, 8 * g : 8 * g + 8, :], out_sem.at[g])

    last = pltpu.make_async_copy(gat.at[G - 1], xb, in_sem)
    last.start()
    for g in range(G - 1):
        result(g).start()
    ends = [
        pltpu.make_async_copy(anom, anom_out, fin_sem.at[0]),
        pltpu.make_async_copy(asset, asset_out, fin_sem.at[1]),
    ]
    for cp in ends:
        cp.start()
    taps.wait()
    last.wait()
    filter_dates(xb, fb, xb, temp)
    result(G - 1).start()
    for cp in ends:
        cp.wait()
    for g in range(G):
        result(g).wait()


def shards(stack, spatial_taps, temporal_taps, foot_tile, foot_row, foot_count, foot_owner):
    anywhere = pl.BlockSpec(memory_space=pl.ANY)
    hbm = pl.BlockSpec(memory_space=pltpu.HBM)
    vm, dma = pltpu.VMEM, pltpu.SemaphoreType.DMA
    sm = pltpu.SMEM
    scratch = [
        sm((2 * RAD + 1,), F32), sm((2, 5), F32), vm((G, TL, 24, C), F32), vm((ND + 2, TL, 8, CB), F32),
        vm((CB, CB), BF16), vm((CB, CB), BF16), vm((CB, CB), BF16), vm((CB, CB), BF16),
        vm((ND, G, TL, 8, CB), F32), vm((G, T, 8, CB), F32), vm((T, 8, CB), F32),
        vm((4, 1, F), I32), vm((ND, 4, 1, F), I32),
        vm((F, F), F32), vm((F, F), F32), vm((F, F), F32), vm((F, F), F32),
        vm((ND, NS, F), F32), vm((8 * F, 8 * F), BF16), vm((8 * F, 8 * F), BF16),
        vm((NS, 1, 9 * F), F32), vm((NS, 1, 9 * F), F32), vm((NS, 9 * F), F32),
        vm((2 * F, F), F32), vm((T, 2 * F), F32), vm((1, F), F32),
        dma((2,)), dma((G + 1,)), dma((4,)), dma((2,)), dma((2,)), dma((ND,)), dma((ND,)),
        dma((G + 1, ND)), dma((G + 1, ND)), dma((ND,)), dma((ND,)), dma((NS,)), dma((NS,)),
        dma((G,)), dma((G,)), dma((2,)),
        pltpu.SemaphoreType.REGULAR, pltpu.SemaphoreType.REGULAR,
    ]
    held = [
        pltpu.with_memory_space_constraint(a, pltpu.HBM)
        for a in (
            stack, spatial_taps, temporal_taps, foot_tile.reshape(1, F), foot_row.reshape(1, F),
            foot_count.reshape(1, F), foot_owner.reshape(1, F),
        )
    ]
    gathered, anomaly, asset = pl.pallas_call(
        kernel,
        out_shape=(
            jax.ShapeDtypeStruct((G, T, 8, CB), F32),
            jax.ShapeDtypeStruct((T, 2 * F), F32),
            jax.ShapeDtypeStruct((1, F), F32),
        ),
        in_specs=[hbm] * 7,
        out_specs=(anywhere, anywhere, anywhere),
        scratch_shapes=scratch,
        compiler_params=pltpu.CompilerParams(
            collective_id=0, has_side_effects=True, vmem_limit_bytes=44 << 20
        ),
        name="series",
    )(*held)
    residual, anomaly, asset = pl.pallas_call(
        finish_kernel,
        out_shape=(
            jax.ShapeDtypeStruct((T, R, CB), F32),
            jax.ShapeDtypeStruct((T, 2 * F), F32),
            jax.ShapeDtypeStruct((1, F), F32),
        ),
        in_specs=[anywhere] * 4,
        out_specs=(hbm, hbm, hbm),
        scratch_shapes=[
            sm((2, 5), F32), vm((T, 8, CB), F32), vm((T, 8, CB), F32), dma, dma, dma((G,)), dma((2,))
        ],
        compiler_params=pltpu.CompilerParams(vmem_limit_bytes=4 << 20),
        name="finish",
    )(gathered, anomaly, asset, temporal_taps)
    return residual, anomaly.T[None], asset[:, :T]


def solution(mesh):
    rows = P(("date", "strip"))
    return jax.shard_map(
        shards,
        mesh=mesh,
        in_specs=(P("date", "strip", None), P(), P(), rows, rows, rows, P(("date", "strip"), None)),
        out_specs=(P(None, "strip", "date"), P(("date", "strip"), None, None), P(("date", "strip"), None)),
        check_vma=False,
    )
```

```python
import functools
import jax
import jax.numpy as jnp
from jax import lax
from jax.experimental import pallas as pl
from jax.experimental.pallas import tpu as pltpu
from jax.sharding import PartitionSpec as P

MESH = pl.DeviceIdType.MESH
F32, BF16, I32 = jnp.float32, jnp.bfloat16, jnp.int32
ND, NS = 8, 16
T, TL = 64, 8
R, G = 64, 8
C, CB, NL = 2048, 256, 16
F = 128
RAD = 6
HT = 4


def dot(a, b):
    return jnp.dot(a, b, preferred_element_type=F32)


def split(x):
    hi = x.astype(BF16)
    return hi, (x - hi.astype(F32)).astype(BF16)


def iota(shape, dim):
    return lax.broadcasted_iota(I32, shape, dim)


def filter_dates(src, mid, dst, temp):
    ca = [-temp[0, k] for k in range(5)]
    cb = [-temp[1, k] for k in range(5)]
    ca[2], cb[2] = 1.0 + ca[2], 1.0 + cb[2]
    for a, b, coef, step in ((src, mid, ca, 1), (mid, dst, cb, 8)):
        for t in range(T):
            acc = coef[2] * a[t]
            for k in (0, 1, 3, 4):
                u = t + step * (k - 2)
                if 0 <= u < T:
                    acc = acc + coef[k] * a[u]
            b[t] = acc


def kernel(
    stack, spat_in, temp_in, ftile, frow, fcount, fowner,
    gat_out, anom_out, asset_out,
    spat, temp, win, rp, b0h, b0l, b1h, b1l, sbuf, rbuf, fbuf,
    mloc, mall, out_t, cnt_t, cnt_o, obuf, st1, wh, wl, y2, z2, zz, xbuf, abuf, asbuf,
    tap_sem, win_sem, ml_sem, halo_s, halo_r, meta_s, meta_r, bulk_s, bulk_r,
    st1_s, st1_r, st2_s, st2_r, keep_sem, out_sem, fin_sem, group_in, all_in,
):
    d = lax.axis_index("date")
    s = lax.axis_index("strip")

    bar = pltpu.get_barrier_semaphore()
    for k in range(1, ND):
        pl.semaphore_signal(bar, inc=1, device_id=((d + k) % ND, s), device_id_type=MESH)

    @pl.when(d == 0)
    def _():
        for k in range(1, NS):
            pl.semaphore_signal(bar, inc=1, device_id=(0, (s + k) % NS), device_id_type=MESH)

    def window(g):
        return [
            pltpu.make_async_copy(
                stack.at[:, g + j], win.at[g, :, :, 8 + 8 * j : 16 + 8 * j, :], win_sem.at[g, j + 1]
            )
            for j in (-1, 0, 1)
            if 0 <= g + j < G
        ]

    def early(h):
        dates, g = slice(HT * h, HT * h + HT), order[0]
        return [
            pltpu.make_async_copy(
                stack.at[dates, g + j],
                win.at[g, dates, :, 8 + 8 * j : 16 + 8 * j, :],
                win_sem.at[G if h else g, j + 1],
            )
            for j in (-1, 0, 1)
        ]

    order = [(i + 1) % G for i in range(G)]
    taps = [
        pltpu.make_async_copy(spat_in, spat, tap_sem.at[0]),
        pltpu.make_async_copy(temp_in, temp, tap_sem.at[1]),
    ]
    for cp in taps:
        cp.start()
    for cp in early(0) + early(1):
        cp.start()
    metas = [
        pltpu.make_async_copy(ref, mloc.at[i], ml_sem.at[i])
        for i, ref in enumerate((ftile, frow, fcount, fowner))
    ]
    for cp in metas:
        cp.start()

    for cp in taps:
        cp.wait()

    total = spat[0]
    for k in range(1, 2 * RAD + 1):
        total = total + spat[k]
    tot = jnp.full((8, CB), total, F32)
    scale = 1.0 / (tot * tot)
    for q in range(CB // 8):
        row = iota((8, CB), 0) + 8 * q
        col = iota((8, CB), 1)
        main = row - col + RAD
        edge = jnp.where(row < 128, row - 128, row + 128) - col + RAD
        vm, ve = jnp.zeros((8, CB), F32), jnp.zeros((8, CB), F32)
        has_edge = 120 <= 8 * q < 136
        for k in range(2 * RAD + 1):
            vm = jnp.where(main == k, spat[k], vm)
            if has_edge:
                ve = jnp.where(edge == k, spat[k], ve)
        fbuf[q] = vm * scale
        fbuf[32 + q] = ve * scale
    h, l = split(fbuf[0:32].reshape(CB, CB))
    b0h[...], b0l[...] = h, l
    h, l = split(fbuf[32:64].reshape(CB, CB))
    b1h[...], b1l[...] = h, l
    rp[0] = jnp.zeros((TL, 8, CB), F32)
    rp[ND + 1] = jnp.zeros((TL, 8, CB), F32)

    def filter_chunk(g, first=None):
        t0, nt = (0, TL) if first is None else (first, HT)
        dates = slice(t0, t0 + nt)

        def row_pass(t, carry):
            for n in range(NL):
                acc = spat[0] * win[g, t, n, 2:10, :]
                for k in range(1, 2 * RAD + 1):
                    acc = acc + spat[k] * win[g, t, n, 2 + k : 10 + k, :]
                rp[n // 2 + 1, t, :, (n % 2) * 128 : (n % 2) * 128 + 128] = acc
            return carry

        lax.fori_loop(t0, t0 + nt, row_pass, 0)
        x = rp[1 : ND + 1, dates].reshape(ND * nt * 8, CB)
        xh, xl = split(x)
        low = dot(xh, b0h[...]) + dot(xl, b0h[...]) + dot(xh, b0l[...])
        e = jnp.concatenate([rp[0:ND, dates, :, 128:], rp[2 : ND + 2, dates, :, :128]], axis=-1)
        eh, el = split(e.reshape(ND * nt * 8, CB))
        low = low + dot(eh, b1h[...]) + dot(el, b1h[...]) + dot(eh, b1l[...])
        low = low.reshape(ND, nt, 8, CB)
        for p in range(ND):
            for n in range(2):
                lanes = slice(n * 128, n * 128 + 128)
                sbuf[p, g, dates, :, lanes] = win[g, dates, 2 * p + n, 8:16, :] - low[p, :, :, lanes]

    def bulk(g, k, into=rbuf):
        p = (d + k) % ND
        return pltpu.make_async_remote_copy(
            src_ref=sbuf.at[p, g],
            dst_ref=into.at[g, pl.ds(TL * d, TL)],
            send_sem=bulk_s.at[g, k],
            recv_sem=bulk_r.at[g, k],
            device_id=(p, s),
            device_id_type=MESH,
        )

    def pair(g, k):
        p = (d + k) % ND
        return pltpu.make_async_remote_copy(
            src_ref=sbuf.at[p, pl.ds(g, 2)],
            dst_ref=rbuf.at[pl.ds(g, 2), pl.ds(TL * d, TL)],
            send_sem=bulk_s.at[g, k],
            recv_sem=bulk_r.at[g, k],
            device_id=(p, s),
            device_id_type=MESH,
        )

    def half(h, k):
        g, p = order[0], (d + k) % ND
        return pltpu.make_async_remote_copy(
            src_ref=sbuf.at[p, g, pl.ds(HT * h, HT)],
            dst_ref=rbuf.at[g, pl.ds(TL * d + HT * h, HT)],
            send_sem=bulk_s.at[g if h else G, k],
            recv_sem=bulk_r.at[g if h else G, k],
            device_id=(p, s),
            device_id_type=MESH,
        )

    def send_half(h):
        for k in range(1, ND):
            half(h, k).start()

    def send_chunk(g, into=rbuf):
        for k in range(1, ND):
            bulk(g, k, into).start()

    def keep(g, into=rbuf):
        return pltpu.make_async_copy(
            sbuf.at[d, g], into.at[g, pl.ds(TL * d, TL)], keep_sem.at[g]
        )

    def halo(down):
        src = stack.at[:, G - 1] if down else stack.at[:, 0]
        dst = win.at[0, :, :, 0:8, :] if down else win.at[G - 1, :, :, 16:24, :]
        i = 0 if down else 1
        to = (s + 1) % NS if down else (s + NS - 1) % NS
        return pltpu.make_async_remote_copy(
            src_ref=src, dst_ref=dst, send_sem=halo_s.at[i], recv_sem=halo_r.at[i],
            device_id=(d, to), device_id_type=MESH,
        )

    def meta(k):
        return pltpu.make_async_remote_copy(
            src_ref=mloc, dst_ref=mall.at[d], send_sem=meta_s.at[k], recv_sem=meta_r.at[k],
            device_id=((d + k) % ND, s), device_id_type=MESH,
        )

    def wait_window(g):
        for j in (-1, 0, 1):
            pltpu.make_async_copy(
                stack.at[:, g + j], win.at[g, :, :, 8 + 8 * j : 16 + 8 * j, :], win_sem.at[g, j + 1]
            ).wait()

    for cp in early(0):
        cp.wait()
    filter_chunk(order[0], 0)
    pl.semaphore_wait(bar, jnp.where(d == 0, ND - 1 + NS - 1, ND - 1))
    send_half(0)
    for g in order[1:]:
        for cp in window(g):
            cp.start()

    @pl.when(d == 0)
    def _():
        for k in range(1, NS):
            pl.semaphore_signal(group_in, inc=1, device_id=(0, (s + k) % NS), device_id_type=MESH)

    for cp in early(1):
        cp.wait()
    filter_chunk(order[0], HT)
    send_half(1)
    for cp in metas:
        cp.wait()
    for k in range(1, ND):
        meta(k).start()

    def interior(g, carry):
        wait_window(g)
        filter_chunk(g)
        return carry

    def two(i, carry):
        lax.fori_loop(3 + 2 * i, 5 + 2 * i, interior, 0)
        for k in range(1, ND):
            pair(3 + 2 * i, k).start()
        return carry

    lax.fori_loop(2, 3, interior, 0)
    send_chunk(2)

    @pl.when(d == 0)
    def _():
        pl.semaphore_wait(group_in, NS - 1)
        for k in range(1, ND):
            pl.semaphore_signal(all_in, inc=1, device_id=(k, s), device_id_type=MESH)

    lax.fori_loop(0, 1, two, 0)

    @pl.when(d != 0)
    def _():
        pl.semaphore_wait(all_in, 1)

    halo(True).start()
    halo(False).start()

    lax.fori_loop(1, 2, two, 0)

    r_, c_ = iota((T, T), 0), iota((T, T), 1)
    r2, c2 = iota((T, 2 * T), 0), iota((T, 2 * T), 1) % T
    near = jnp.where(r_ == c_, 1.0, 0.0).astype(F32)
    far = jnp.where(r2 == c2, 1.0, 0.0).astype(F32)
    for k in range(5):
        near = near - jnp.where(r_ - c_ == k - 2, temp[0, k], 0.0)
        far = far - jnp.where(r2 - c2 == 8 * (k - 2), temp[1, k], 0.0)
    tt = jnp.dot(near, far, precision=lax.Precision.HIGHEST, preferred_element_type=F32)
    wh[...] = jnp.zeros(wh.shape, BF16)
    wl[...] = jnp.zeros(wl.shape, BF16)
    left = iota((8, 2 * T), 1) < T
    for i in range(ND):
        part = tt[8 * i : 8 * i + 8]
        base = jnp.concatenate([jnp.where(left, part, 0.0), jnp.where(left, 0.0, part)], axis=0)
        bh, bl = split(base)
        for p in range(ND):
            wh[i * 128 + 16 * p : i * 128 + 16 * p + 16, 128 * p : 128 * p + 128] = bh
            wl[i * 128 + 16 * p : i * 128 + 16 * p + 16, 128 * p : 128 * p + 128] = bl

    halo(True).wait()
    halo(False).wait()
    for g in (0, G - 1):
        for cp in window(g):
            cp.wait()

    @pl.when(s == 0)
    def _():
        win[0, :, :, 0:8, :] = jnp.zeros((TL, NL, 8, 128), F32)

    @pl.when(s == NS - 1)
    def _():
        win[G - 1, :, :, 16:24, :] = jnp.zeros((TL, NL, 8, 128), F32)

    def edge_chunk(i, carry):
        filter_chunk((G - 1) * i)
        return carry

    lax.fori_loop(0, 2, edge_chunk, 0)

    mall[d] = mloc[...]
    for k in range(1, ND):
        meta(k).wait()
    cnt_t[...] = jnp.zeros(cnt_t.shape, F32)

    def block(p, carry):
        tile, row, count, owner = (mall[p, i] for i in range(4))
        jj = iota((CB, F), 0)
        inside = ((jj >> 7) == tile) & ((jj & 127) < count)
        m = jnp.where(inside, 1.0, 0.0).astype(BF16)
        xh, xl = split(sbuf[p].reshape(G * TL * 8, CB))
        g_ = (dot(xh, m) + dot(xl, m)).reshape(G, TL, 8, F)
        here = iota((G, 8, F), 0) * 8 + iota((G, 8, F), 1) == row.reshape(1, 1, F)
        picked = jnp.sum(jnp.where(here[:, None], g_, 0.0), axis=0)
        cf = count.astype(F32)
        mean = jnp.sum(picked, axis=1) / cf
        own = jnp.broadcast_to(owner.astype(F32), (F, F))
        own_t = own.T
        sub, lane = iota((F, F), 0), iota((F, F), 1)
        earlier = (own == own_t) & (sub < lane)
        slot = jnp.sum(jnp.where(earlier, 1.0, 0.0), axis=0, keepdims=True)
        onehot = jnp.where(own_t == lane.astype(F32), 1.0, 0.0)
        rows = jnp.concatenate(
            [
                jnp.where(slot == 0.0, mean, 0.0),
                jnp.where(slot == 1.0, mean, 0.0),
                jnp.where(iota((8, F), 0).astype(F32) == slot, cf, 0.0),
            ],
            axis=0,
        )
        got = jnp.dot(rows, onehot, precision=lax.Precision.HIGHEST, preferred_element_type=F32)
        out_t[pl.ds(pl.multiple_of(16 * p, 16), 16)] = got[0:16]
        cnt_t[pl.ds(pl.multiple_of(8 * p, 8), 8)] = got[16:24]
        return carry

    lax.fori_loop(0, ND, block, 0)
    obuf[...] = out_t[...].T
    cnt_o[...] = cnt_t[...].T

    def stage1(k):
        p = (d + k) % ND
        return pltpu.make_async_remote_copy(
            src_ref=obuf.at[pl.ds(pl.multiple_of(16 * p, 16), 16)], dst_ref=st1.at[d],
            send_sem=st1_s.at[k], recv_sem=st1_r.at[k],
            device_id=(p, s), device_id_type=MESH,
        )

    for k in range(1, ND):
        stage1(k).start()
    mine = pl.ds(pl.multiple_of(16 * d, 16), 16)
    st1[d] = obuf[mine]
    send_chunk(0)
    send_chunk(G - 1, gat_out)
    for g in range(G - 1):
        keep(g).start()
    keep(G - 1, gat_out).start()

    def result(g):
        return pltpu.make_async_copy(rbuf.at[g], gat_out.at[g], out_sem.at[g])

    def complete(g):
        filter_dates(rbuf.at[g], fbuf, rbuf.at[g], temp)
        result(g).start()

    def finish_single(i, carry):
        g = 2 - 2 * i
        keep(g).wait()
        for k in range(1, ND):
            bulk(g, k).wait()
        complete(g)
        return carry

    def finish_two(i, carry):
        g = 3 + 2 * i
        for k in range(1, ND):
            pair(g, k).wait()
        for j in range(2):
            keep(g + j).wait()
        lax.fori_loop(g, g + 2, finish_one, 0)
        return carry

    def finish_one(g, carry):
        complete(g)
        return carry

    keep(order[0]).wait()
    for k in range(1, ND):
        half(0, k).wait()
        half(1, k).wait()
    lax.fori_loop(order[0], order[0] + 1, finish_one, 0)
    lax.fori_loop(0, 1, finish_single, 0)
    lax.fori_loop(0, 2, finish_two, 0)

    for k in range(1, ND):
        stage1(k).wait()
    ser = jnp.concatenate([st1[i] for i in range(ND)], axis=-1)
    sh, sl = split(ser)
    y = dot(sh, wh[...]) + dot(sl, wh[...]) + dot(sh, wl[...])
    cnt = cnt_o[mine]
    for i in range(NS):
        y2[i, :, 0 : 8 * F] = y[i : i + 1]
        y2[i, :, 8 * F : 9 * F] = cnt[i : i + 1]

    def stage2(k):
        o = (s + k) % NS
        return pltpu.make_async_remote_copy(
            src_ref=y2.at[o], dst_ref=z2.at[s],
            send_sem=st2_s.at[k], recv_sem=st2_r.at[k],
            device_id=(d, o), device_id_type=MESH,
        )

    for k in range(1, NS):
        stage2(k).start()
    z2[s] = y2[s]

    lax.fori_loop(1, 2, finish_single, 0)

    for k in range(1, NS):
        stage2(k).wait()
    for i in range(NS):
        zz[i : i + 1] = z2[i]
    z, cn = zz[:, 0 : 8 * F], zz[:, 8 * F : 9 * F]
    spread = jnp.where(
        iota((F, 8 * F), 0) == (iota((F, 8 * F), 1) // F) * 8 + (iota((F, 8 * F), 1) % F) // T, 1.0, 0.0
    ).astype(BF16)
    weight = dot(cn.astype(BF16), spread)
    part = jnp.sum(weight * z, axis=0, keepdims=True)
    acc = part[:, 0:F]
    for i in range(1, ND):
        acc = acc + part[:, i * F : (i + 1) * F]
    acc = acc + jnp.concatenate([acc[:, T:], acc[:, :T]], axis=1)
    asset = acc / jnp.sum(cn)
    for i in range(ND):
        cols = slice(i * F, (i + 1) * F)
        anom = jnp.where(weight[:, cols] > 0, z[:, cols] - asset, 0.0)
        xbuf[pl.ds(32 * i, NS, stride=2)] = anom
        xbuf[pl.ds(32 * i + 1, NS, stride=2)] = pltpu.roll(anom, T, 1)
    abuf[...] = xbuf[...].T[0:T]
    asbuf[...] = asset
    ends = [
        pltpu.make_async_copy(abuf, anom_out, fin_sem.at[0]),
        pltpu.make_async_copy(asbuf, asset_out, fin_sem.at[1]),
    ]
    for cp in ends:
        cp.start()
    for cp in ends:
        cp.wait()
    for g in range(G - 1):
        result(g).wait()
    keep(G - 1, gat_out).wait()
    for k in range(1, ND):
        bulk(G - 1, k, gat_out).wait()


def finish_kernel(
    gat, anom, asset, temp_in, res_out, anom_out, asset_out, temp, xb, fb, in_sem, tap_sem, out_sem, fin_sem
):
    taps = pltpu.make_async_copy(temp_in, temp, tap_sem)
    taps.start()

    def result(g):
        src = gat.at[g] if g < G - 1 else xb
        return pltpu.make_async_copy(src, res_out.at[:, 8 * g : 8 * g + 8, :], out_sem.at[g])

    last = pltpu.make_async_copy(gat.at[G - 1], xb, in_sem)
    last.start()
    for g in range(G - 1):
        result(g).start()
    ends = [
        pltpu.make_async_copy(anom, anom_out, fin_sem.at[0]),
        pltpu.make_async_copy(asset, asset_out, fin_sem.at[1]),
    ]
    for cp in ends:
        cp.start()
    taps.wait()
    last.wait()
    filter_dates(xb, fb, xb, temp)
    result(G - 1).start()
    for cp in ends:
        cp.wait()
    for g in range(G):
        result(g).wait()


def shards(stack, spatial_taps, temporal_taps, foot_tile, foot_row, foot_count, foot_owner):
    anywhere = pl.BlockSpec(memory_space=pl.ANY)
    hbm = pl.BlockSpec(memory_space=pltpu.HBM)
    vm, dma = pltpu.VMEM, pltpu.SemaphoreType.DMA
    sm = pltpu.SMEM
    scratch = [
        sm((2 * RAD + 1,), F32), sm((2, 5), F32), vm((G, TL, NL, 24, 128), F32), vm((ND + 2, TL, 8, CB), F32),
        vm((CB, CB), BF16), vm((CB, CB), BF16), vm((CB, CB), BF16), vm((CB, CB), BF16),
        vm((ND, G, TL, 8, CB), F32), vm((G, T, 8, CB), F32), vm((T, 8, CB), F32),
        vm((4, 1, F), I32), vm((ND, 4, 1, F), I32),
        vm((F, F), F32), vm((F, F), F32), vm((F, F), F32), vm((F, F), F32),
        vm((ND, NS, F), F32), vm((8 * F, 8 * F), BF16), vm((8 * F, 8 * F), BF16),
        vm((NS, 1, 9 * F), F32), vm((NS, 1, 9 * F), F32), vm((NS, 9 * F), F32),
        vm((2 * F, F), F32), vm((T, 2 * F), F32), vm((1, F), F32),
        dma((2,)), dma((G + 1, 3)), dma((4,)), dma((2,)), dma((2,)), dma((ND,)), dma((ND,)),
        dma((G + 1, ND)), dma((G + 1, ND)), dma((ND,)), dma((ND,)), dma((NS,)), dma((NS,)),
        dma((G,)), dma((G,)), dma((2,)),
        pltpu.SemaphoreType.REGULAR, pltpu.SemaphoreType.REGULAR,
    ]
    held = [
        pltpu.with_memory_space_constraint(a, pltpu.HBM)
        for a in (
            stack.reshape(TL, G, 8, NL, 128).swapaxes(2, 3), spatial_taps, temporal_taps, foot_tile.reshape(1, F), foot_row.reshape(1, F),
            foot_count.reshape(1, F), foot_owner.reshape(1, F),
        )
    ]
    gathered, anomaly, asset = pl.pallas_call(
        kernel,
        out_shape=(
            jax.ShapeDtypeStruct((G, T, 8, CB), F32),
            jax.ShapeDtypeStruct((T, 2 * F), F32),
            jax.ShapeDtypeStruct((1, F), F32),
        ),
        in_specs=[hbm] * 7,
        out_specs=(anywhere, anywhere, anywhere),
        scratch_shapes=scratch,
        compiler_params=pltpu.CompilerParams(
            collective_id=0, has_side_effects=True, vmem_limit_bytes=44 << 20
        ),
        name="series",
    )(*held)
    residual, anomaly, asset = pl.pallas_call(
        finish_kernel,
        out_shape=(
            jax.ShapeDtypeStruct((T, R, CB), F32),
            jax.ShapeDtypeStruct((T, 2 * F), F32),
            jax.ShapeDtypeStruct((1, F), F32),
        ),
        in_specs=[anywhere] * 4,
        out_specs=(hbm, hbm, hbm),
        scratch_shapes=[
            sm((2, 5), F32), vm((T, 8, CB), F32), vm((T, 8, CB), F32), dma, dma, dma((G,)), dma((2,))
        ],
        compiler_params=pltpu.CompilerParams(vmem_limit_bytes=4 << 20),
        name="finish",
    )(gathered, anomaly, asset, temporal_taps)
    return residual, anomaly.T[None], asset[:, :T]


def solution(mesh):
    rows = P(("date", "strip"))
    return jax.shard_map(
        shards,
        mesh=mesh,
        in_specs=(P("date", "strip", None), P(), P(), rows, rows, rows, P(("date", "strip"), None)),
        out_specs=(P(None, "strip", "date"), P(("date", "strip"), None, None), P(("date", "strip"), None)),
        check_vma=False,
    )
```

```python
import functools
import jax
import jax.numpy as jnp
from jax import lax
from jax.experimental import pallas as pl
from jax.experimental.pallas import tpu as pltpu
from jax.sharding import PartitionSpec as P

MESH = pl.DeviceIdType.MESH
F32, BF16, I32 = jnp.float32, jnp.bfloat16, jnp.int32
ND, NS = 8, 16
T, TL = 64, 8
R, G = 64, 8
C, CB, NL = 2048, 256, 16
F = 128
RAD = 6
FAR_FIRST = (4, 5, 2, 6, 3, 7, 1)
HT = 4


def dot(a, b):
    return jnp.dot(a, b, preferred_element_type=F32)


def split(x):
    hi = x.astype(BF16)
    return hi, (x - hi.astype(F32)).astype(BF16)


def iota(shape, dim):
    return lax.broadcasted_iota(I32, shape, dim)


def filter_dates(src, mid, dst, temp):
    ca = [-temp[0, k] for k in range(5)]
    cb = [-temp[1, k] for k in range(5)]
    ca[2], cb[2] = 1.0 + ca[2], 1.0 + cb[2]
    for a, b, coef, step in ((src, mid, ca, 1), (mid, dst, cb, 8)):
        for t in range(T):
            acc = coef[2] * a[t]
            for k in (0, 1, 3, 4):
                u = t + step * (k - 2)
                if 0 <= u < T:
                    acc = acc + coef[k] * a[u]
            b[t] = acc


def kernel(
    stack, spat_in, temp_in, ftile, frow, fcount, fowner,
    gat_out, anom_out, asset_out,
    spat, temp, win, rp, b0h, b0l, b1h, b1l, sbuf, rbuf, fbuf,
    mloc, mall, out_t, cnt_t, cnt_o, obuf, st1, wh, wl, y2, z2, zz, xbuf, abuf, asbuf,
    tap_sem, win_sem, ml_sem, halo_s, halo_r, meta_s, meta_r, bulk_s, bulk_r,
    st1_s, st1_r, st2_s, st2_r, keep_sem, out_sem, fin_sem, group_in, all_in,
):
    d = lax.axis_index("date")
    s = lax.axis_index("strip")

    bar = pltpu.get_barrier_semaphore()
    for k in range(1, ND):
        pl.semaphore_signal(bar, inc=1, device_id=((d + k) % ND, s), device_id_type=MESH)

    @pl.when(d == 0)
    def _():
        for k in range(1, NS):
            pl.semaphore_signal(bar, inc=1, device_id=(0, (s + k) % NS), device_id_type=MESH)

    def window(g):
        return [
            pltpu.make_async_copy(
                stack.at[:, g + j], win.at[g, :, :, 8 + 8 * j : 16 + 8 * j, :], win_sem.at[g, j + 1]
            )
            for j in (-1, 0, 1)
            if 0 <= g + j < G
        ]

    def early(h):
        dates, g = slice(HT * h, HT * h + HT), order[0]
        return [
            pltpu.make_async_copy(
                stack.at[dates, g + j],
                win.at[g, dates, :, 8 + 8 * j : 16 + 8 * j, :],
                win_sem.at[G if h else g, j + 1],
            )
            for j in (-1, 0, 1)
        ]

    order = [(i + 1) % G for i in range(G)]
    taps = [
        pltpu.make_async_copy(spat_in, spat, tap_sem.at[0]),
        pltpu.make_async_copy(temp_in, temp, tap_sem.at[1]),
    ]
    for cp in taps:
        cp.start()
    for cp in early(0) + early(1):
        cp.start()
    metas = [
        pltpu.make_async_copy(ref, mloc.at[i], ml_sem.at[i])
        for i, ref in enumerate((ftile, frow, fcount, fowner))
    ]
    for cp in metas:
        cp.start()

    for cp in taps:
        cp.wait()

    total = spat[0]
    for k in range(1, 2 * RAD + 1):
        total = total + spat[k]
    tot = jnp.full((8, CB), total, F32)
    scale = 1.0 / (tot * tot)
    for q in range(CB // 8):
        row = iota((8, CB), 0) + 8 * q
        col = iota((8, CB), 1)
        main = row - col + RAD
        edge = jnp.where(row < 128, row - 128, row + 128) - col + RAD
        vm, ve = jnp.zeros((8, CB), F32), jnp.zeros((8, CB), F32)
        has_edge = 120 <= 8 * q < 136
        for k in range(2 * RAD + 1):
            vm = jnp.where(main == k, spat[k], vm)
            if has_edge:
                ve = jnp.where(edge == k, spat[k], ve)
        fbuf[q] = vm * scale
        fbuf[32 + q] = ve * scale
    h, l = split(fbuf[0:32].reshape(CB, CB))
    b0h[...], b0l[...] = h, l
    h, l = split(fbuf[32:64].reshape(CB, CB))
    b1h[...], b1l[...] = h, l
    rp[0] = jnp.zeros((TL, 8, CB), F32)
    rp[ND + 1] = jnp.zeros((TL, 8, CB), F32)

    def filter_chunk(g, first=None):
        t0, nt = (0, TL) if first is None else (first, HT)
        dates = slice(t0, t0 + nt)

        def row_pass(t, carry):
            for n in range(NL):
                acc = spat[0] * win[g, t, n, 2:10, :]
                for k in range(1, 2 * RAD + 1):
                    acc = acc + spat[k] * win[g, t, n, 2 + k : 10 + k, :]
                rp[n // 2 + 1, t, :, (n % 2) * 128 : (n % 2) * 128 + 128] = acc
            return carry

        lax.fori_loop(t0, t0 + nt, row_pass, 0)
        x = rp[1 : ND + 1, dates].reshape(ND * nt * 8, CB)
        xh, xl = split(x)
        low = dot(xh, b0h[...]) + dot(xl, b0h[...]) + dot(xh, b0l[...])
        e = jnp.concatenate([rp[0:ND, dates, :, 128:], rp[2 : ND + 2, dates, :, :128]], axis=-1)
        eh, el = split(e.reshape(ND * nt * 8, CB))
        low = low + dot(eh, b1h[...]) + dot(el, b1h[...]) + dot(eh, b1l[...])
        low = low.reshape(ND, nt, 8, CB)
        for p in range(ND):
            for n in range(2):
                lanes = slice(n * 128, n * 128 + 128)
                sbuf[p, g, dates, :, lanes] = win[g, dates, 2 * p + n, 8:16, :] - low[p, :, :, lanes]

    def peer(k):
        return (d // 2 + k // 2) % (ND // 2) * 2 + (d + k) % 2

    def bulk(g, k, into=rbuf):
        p = peer(k)
        return pltpu.make_async_remote_copy(
            src_ref=sbuf.at[p, g],
            dst_ref=into.at[g, pl.ds(TL * d, TL)],
            send_sem=bulk_s.at[g, k],
            recv_sem=bulk_r.at[g, k],
            device_id=(p, s),
            device_id_type=MESH,
        )

    def pair(g, k):
        p = peer(k)
        return pltpu.make_async_remote_copy(
            src_ref=sbuf.at[p, pl.ds(g, 2)],
            dst_ref=rbuf.at[pl.ds(g, 2), pl.ds(TL * d, TL)],
            send_sem=bulk_s.at[g, k],
            recv_sem=bulk_r.at[g, k],
            device_id=(p, s),
            device_id_type=MESH,
        )

    def half(h, k):
        g, p = order[0], peer(k)
        return pltpu.make_async_remote_copy(
            src_ref=sbuf.at[p, g, pl.ds(HT * h, HT)],
            dst_ref=rbuf.at[g, pl.ds(TL * d + HT * h, HT)],
            send_sem=bulk_s.at[g if h else G, k],
            recv_sem=bulk_r.at[g if h else G, k],
            device_id=(p, s),
            device_id_type=MESH,
        )

    def send_half(h):
        for k in FAR_FIRST:
            half(h, k).start()

    def send_chunk(g, into=rbuf):
        for k in FAR_FIRST:
            bulk(g, k, into).start()

    def keep(g, into=rbuf):
        return pltpu.make_async_copy(
            sbuf.at[d, g], into.at[g, pl.ds(TL * d, TL)], keep_sem.at[g]
        )

    def halo(down):
        src = stack.at[:, G - 1] if down else stack.at[:, 0]
        dst = win.at[0, :, :, 0:8, :] if down else win.at[G - 1, :, :, 16:24, :]
        i = 0 if down else 1
        to = (s + 1) % NS if down else (s + NS - 1) % NS
        return pltpu.make_async_remote_copy(
            src_ref=src, dst_ref=dst, send_sem=halo_s.at[i], recv_sem=halo_r.at[i],
            device_id=(d, to), device_id_type=MESH,
        )

    def meta(k):
        return pltpu.make_async_remote_copy(
            src_ref=mloc, dst_ref=mall.at[d], send_sem=meta_s.at[k], recv_sem=meta_r.at[k],
            device_id=((d + k) % ND, s), device_id_type=MESH,
        )

    def wait_window(g):
        for j in (-1, 0, 1):
            pltpu.make_async_copy(
                stack.at[:, g + j], win.at[g, :, :, 8 + 8 * j : 16 + 8 * j, :], win_sem.at[g, j + 1]
            ).wait()

    for cp in early(0):
        cp.wait()
    filter_chunk(order[0], 0)
    pl.semaphore_wait(bar, jnp.where(d == 0, ND - 1 + NS - 1, ND - 1))
    send_half(0)
    for g in order[1:]:
        for cp in window(g):
            cp.start()

    @pl.when(d == 0)
    def _():
        for k in range(1, NS):
            pl.semaphore_signal(group_in, inc=1, device_id=(0, (s + k) % NS), device_id_type=MESH)

    for cp in early(1):
        cp.wait()
    filter_chunk(order[0], HT)
    send_half(1)
    for cp in metas:
        cp.wait()
    for k in range(1, ND):
        meta(k).start()

    def interior(g, carry):
        wait_window(g)
        filter_chunk(g)
        return carry

    def two(i, carry):
        lax.fori_loop(3 + 2 * i, 5 + 2 * i, interior, 0)
        for k in FAR_FIRST:
            pair(3 + 2 * i, k).start()
        return carry

    lax.fori_loop(2, 3, interior, 0)
    send_chunk(2)

    @pl.when(d == 0)
    def _():
        pl.semaphore_wait(group_in, NS - 1)
        for k in range(1, ND):
            pl.semaphore_signal(all_in, inc=1, device_id=(k, s), device_id_type=MESH)

    lax.fori_loop(0, 1, two, 0)

    @pl.when(d != 0)
    def _():
        pl.semaphore_wait(all_in, 1)

    halo(True).start()
    halo(False).start()

    lax.fori_loop(1, 2, two, 0)

    r_, c_ = iota((T, T), 0), iota((T, T), 1)
    r2, c2 = iota((T, 2 * T), 0), iota((T, 2 * T), 1) % T
    near = jnp.where(r_ == c_, 1.0, 0.0).astype(F32)
    far = jnp.where(r2 == c2, 1.0, 0.0).astype(F32)
    for k in range(5):
        near = near - jnp.where(r_ - c_ == k - 2, temp[0, k], 0.0)
        far = far - jnp.where(r2 - c2 == 8 * (k - 2), temp[1, k], 0.0)
    tt = jnp.dot(near, far, precision=lax.Precision.HIGHEST, preferred_element_type=F32)
    wh[...] = jnp.zeros(wh.shape, BF16)
    wl[...] = jnp.zeros(wl.shape, BF16)
    left = iota((8, 2 * T), 1) < T
    for i in range(ND):
        part = tt[8 * i : 8 * i + 8]
        base = jnp.concatenate([jnp.where(left, part, 0.0), jnp.where(left, 0.0, part)], axis=0)
        bh, bl = split(base)
        for p in range(ND):
            wh[i * 128 + 16 * p : i * 128 + 16 * p + 16, 128 * p : 128 * p + 128] = bh
            wl[i * 128 + 16 * p : i * 128 + 16 * p + 16, 128 * p : 128 * p + 128] = bl

    halo(True).wait()
    halo(False).wait()
    for g in (0, G - 1):
        for cp in window(g):
            cp.wait()

    @pl.when(s == 0)
    def _():
        win[0, :, :, 0:8, :] = jnp.zeros((TL, NL, 8, 128), F32)

    @pl.when(s == NS - 1)
    def _():
        win[G - 1, :, :, 16:24, :] = jnp.zeros((TL, NL, 8, 128), F32)

    def edge_chunk(i, carry):
        filter_chunk((G - 1) * i)
        return carry

    lax.fori_loop(0, 2, edge_chunk, 0)

    mall[d] = mloc[...]
    for k in range(1, ND):
        meta(k).wait()
    cnt_t[...] = jnp.zeros(cnt_t.shape, F32)

    def block(p, carry):
        tile, row, count, owner = (mall[p, i] for i in range(4))
        jj = iota((CB, F), 0)
        inside = ((jj >> 7) == tile) & ((jj & 127) < count)
        m = jnp.where(inside, 1.0, 0.0).astype(BF16)
        xh, xl = split(sbuf[p].reshape(G * TL * 8, CB))
        g_ = (dot(xh, m) + dot(xl, m)).reshape(G, TL, 8, F)
        here = iota((G, 8, F), 0) * 8 + iota((G, 8, F), 1) == row.reshape(1, 1, F)
        picked = jnp.sum(jnp.where(here[:, None], g_, 0.0), axis=0)
        cf = count.astype(F32)
        mean = jnp.sum(picked, axis=1) / cf
        own = jnp.broadcast_to(owner.astype(F32), (F, F))
        own_t = own.T
        sub, lane = iota((F, F), 0), iota((F, F), 1)
        earlier = (own == own_t) & (sub < lane)
        slot = jnp.sum(jnp.where(earlier, 1.0, 0.0), axis=0, keepdims=True)
        onehot = jnp.where(own_t == lane.astype(F32), 1.0, 0.0)
        rows = jnp.concatenate(
            [
                jnp.where(slot == 0.0, mean, 0.0),
                jnp.where(slot == 1.0, mean, 0.0),
                jnp.where(iota((8, F), 0).astype(F32) == slot, cf, 0.0),
            ],
            axis=0,
        )
        got = jnp.dot(rows, onehot, precision=lax.Precision.HIGHEST, preferred_element_type=F32)
        out_t[pl.ds(pl.multiple_of(16 * p, 16), 16)] = got[0:16]
        cnt_t[pl.ds(pl.multiple_of(8 * p, 8), 8)] = got[16:24]
        return carry

    lax.fori_loop(0, ND, block, 0)
    obuf[...] = out_t[...].T
    cnt_o[...] = cnt_t[...].T

    def stage1(k):
        p = (d + k) % ND
        return pltpu.make_async_remote_copy(
            src_ref=obuf.at[pl.ds(pl.multiple_of(16 * p, 16), 16)], dst_ref=st1.at[d],
            send_sem=st1_s.at[k], recv_sem=st1_r.at[k],
            device_id=(p, s), device_id_type=MESH,
        )

    for k in range(1, ND):
        stage1(k).start()
    mine = pl.ds(pl.multiple_of(16 * d, 16), 16)
    st1[d] = obuf[mine]
    send_chunk(0)
    send_chunk(G - 1, gat_out)
    for g in range(G - 1):
        keep(g).start()
    keep(G - 1, gat_out).start()

    def result(g):
        return pltpu.make_async_copy(rbuf.at[g], gat_out.at[g], out_sem.at[g])

    def complete(g):
        filter_dates(rbuf.at[g], fbuf, rbuf.at[g], temp)
        result(g).start()

    def finish_single(i, carry):
        g = 2 - 2 * i
        keep(g).wait()
        for k in range(1, ND):
            bulk(g, k).wait()
        complete(g)
        return carry

    def finish_two(i, carry):
        g = 3 + 2 * i
        for k in range(1, ND):
            pair(g, k).wait()
        for j in range(2):
            keep(g + j).wait()
        lax.fori_loop(g, g + 2, finish_one, 0)
        return carry

    def finish_one(g, carry):
        complete(g)
        return carry

    keep(order[0]).wait()
    for k in range(1, ND):
        half(0, k).wait()
        half(1, k).wait()
    lax.fori_loop(order[0], order[0] + 1, finish_one, 0)
    lax.fori_loop(0, 1, finish_single, 0)
    lax.fori_loop(0, 2, finish_two, 0)

    for k in range(1, ND):
        stage1(k).wait()
    ser = jnp.concatenate([st1[i] for i in range(ND)], axis=-1)
    sh, sl = split(ser)
    y = dot(sh, wh[...]) + dot(sl, wh[...]) + dot(sh, wl[...])
    cnt = cnt_o[mine]
    for i in range(NS):
        y2[i, :, 0 : 8 * F] = y[i : i + 1]
        y2[i, :, 8 * F : 9 * F] = cnt[i : i + 1]

    def stage2(k):
        o = (s + k) % NS
        return pltpu.make_async_remote_copy(
            src_ref=y2.at[o], dst_ref=z2.at[s],
            send_sem=st2_s.at[k], recv_sem=st2_r.at[k],
            device_id=(d, o), device_id_type=MESH,
        )

    for k in range(1, NS):
        stage2(k).start()
    z2[s] = y2[s]

    lax.fori_loop(1, 2, finish_single, 0)

    for k in range(1, NS):
        stage2(k).wait()
    for i in range(NS):
        zz[i : i + 1] = z2[i]
    z, cn = zz[:, 0 : 8 * F], zz[:, 8 * F : 9 * F]
    spread = jnp.where(
        iota((F, 8 * F), 0) == (iota((F, 8 * F), 1) // F) * 8 + (iota((F, 8 * F), 1) % F) // T, 1.0, 0.0
    ).astype(BF16)
    weight = dot(cn.astype(BF16), spread)
    part = jnp.sum(weight * z, axis=0, keepdims=True)
    acc = part[:, 0:F]
    for i in range(1, ND):
        acc = acc + part[:, i * F : (i + 1) * F]
    acc = acc + jnp.concatenate([acc[:, T:], acc[:, :T]], axis=1)
    asset = acc / jnp.sum(cn)
    for i in range(ND):
        cols = slice(i * F, (i + 1) * F)
        anom = jnp.where(weight[:, cols] > 0, z[:, cols] - asset, 0.0)
        xbuf[pl.ds(32 * i, NS, stride=2)] = anom
        xbuf[pl.ds(32 * i + 1, NS, stride=2)] = pltpu.roll(anom, T, 1)
    abuf[...] = xbuf[...].T[0:T]
    asbuf[...] = asset
    ends = [
        pltpu.make_async_copy(abuf, anom_out, fin_sem.at[0]),
        pltpu.make_async_copy(asbuf, asset_out, fin_sem.at[1]),
    ]
    for cp in ends:
        cp.start()
    for cp in ends:
        cp.wait()
    for g in range(G - 1):
        result(g).wait()
    keep(G - 1, gat_out).wait()
    for k in range(1, ND):
        bulk(G - 1, k, gat_out).wait()


def finish_kernel(
    gat, anom, asset, temp_in, res_out, anom_out, asset_out, temp, xb, fb, in_sem, tap_sem, out_sem, fin_sem
):
    taps = pltpu.make_async_copy(temp_in, temp, tap_sem)
    taps.start()

    def result(g):
        src = gat.at[g] if g < G - 1 else xb
        return pltpu.make_async_copy(src, res_out.at[:, 8 * g : 8 * g + 8, :], out_sem.at[g])

    last = pltpu.make_async_copy(gat.at[G - 1], xb, in_sem)
    last.start()
    for g in range(G - 1):
        result(g).start()
    ends = [
        pltpu.make_async_copy(anom, anom_out, fin_sem.at[0]),
        pltpu.make_async_copy(asset, asset_out, fin_sem.at[1]),
    ]
    for cp in ends:
        cp.start()
    taps.wait()
    last.wait()
    filter_dates(xb, fb, xb, temp)
    result(G - 1).start()
    for cp in ends:
        cp.wait()
    for g in range(G):
        result(g).wait()


def shards(stack, spatial_taps, temporal_taps, foot_tile, foot_row, foot_count, foot_owner):
    anywhere = pl.BlockSpec(memory_space=pl.ANY)
    hbm = pl.BlockSpec(memory_space=pltpu.HBM)
    vm, dma = pltpu.VMEM, pltpu.SemaphoreType.DMA
    sm = pltpu.SMEM
    scratch = [
        sm((2 * RAD + 1,), F32), sm((2, 5), F32), vm((G, TL, NL, 24, 128), F32), vm((ND + 2, TL, 8, CB), F32),
        vm((CB, CB), BF16), vm((CB, CB), BF16), vm((CB, CB), BF16), vm((CB, CB), BF16),
        vm((ND, G, TL, 8, CB), F32), vm((G, T, 8, CB), F32), vm((T, 8, CB), F32),
        vm((4, 1, F), I32), vm((ND, 4, 1, F), I32),
        vm((F, F), F32), vm((F, F), F32), vm((F, F), F32), vm((F, F), F32),
        vm((ND, NS, F), F32), vm((8 * F, 8 * F), BF16), vm((8 * F, 8 * F), BF16),
        vm((NS, 1, 9 * F), F32), vm((NS, 1, 9 * F), F32), vm((NS, 9 * F), F32),
        vm((2 * F, F), F32), vm((T, 2 * F), F32), vm((1, F), F32),
        dma((2,)), dma((G + 1, 3)), dma((4,)), dma((2,)), dma((2,)), dma((ND,)), dma((ND,)),
        dma((G + 1, ND)), dma((G + 1, ND)), dma((ND,)), dma((ND,)), dma((NS,)), dma((NS,)),
        dma((G,)), dma((G,)), dma((2,)),
        pltpu.SemaphoreType.REGULAR, pltpu.SemaphoreType.REGULAR,
    ]
    held = [
        pltpu.with_memory_space_constraint(a, pltpu.HBM)
        for a in (
            stack.reshape(TL, G, 8, NL, 128).swapaxes(2, 3), spatial_taps, temporal_taps, foot_tile.reshape(1, F), foot_row.reshape(1, F),
            foot_count.reshape(1, F), foot_owner.reshape(1, F),
        )
    ]
    gathered, anomaly, asset = pl.pallas_call(
        kernel,
        out_shape=(
            jax.ShapeDtypeStruct((G, T, 8, CB), F32),
            jax.ShapeDtypeStruct((T, 2 * F), F32),
            jax.ShapeDtypeStruct((1, F), F32),
        ),
        in_specs=[hbm] * 7,
        out_specs=(anywhere, anywhere, anywhere),
        scratch_shapes=scratch,
        compiler_params=pltpu.CompilerParams(
            collective_id=0, has_side_effects=True, vmem_limit_bytes=44 << 20
        ),
        name="series",
    )(*held)
    residual, anomaly, asset = pl.pallas_call(
        finish_kernel,
        out_shape=(
            jax.ShapeDtypeStruct((T, R, CB), F32),
            jax.ShapeDtypeStruct((T, 2 * F), F32),
            jax.ShapeDtypeStruct((1, F), F32),
        ),
        in_specs=[anywhere] * 4,
        out_specs=(hbm, hbm, hbm),
        scratch_shapes=[
            sm((2, 5), F32), vm((T, 8, CB), F32), vm((T, 8, CB), F32), dma, dma, dma((G,)), dma((2,))
        ],
        compiler_params=pltpu.CompilerParams(vmem_limit_bytes=4 << 20),
        name="finish",
    )(gathered, anomaly, asset, temporal_taps)
    return residual, anomaly.T[None], asset[:, :T]


def solution(mesh):
    rows = P(("date", "strip"))
    return jax.shard_map(
        shards,
        mesh=mesh,
        in_specs=(P("date", "strip", None), P(), P(), rows, rows, rows, P(("date", "strip"), None)),
        out_specs=(P(None, "strip", "date"), P(("date", "strip"), None, None), P(("date", "strip"), None)),
        check_vma=False,
    )
```
